32 devices in a mesh: seq: 8 (over y, x, core), head: 4 (over z).
Axes of the slice: x: 2, y: 2, z: 4, core: 2. Of those that a mesh axis runs over, the one named last changes fastest.
Arguments:
- queries: bfloat16 [2048, 16, 128], P('seq', 'head'), may hold values from -30 to 30
- keys: bfloat16 [2048, 16, 128], P('seq', 'head'), may hold values from -12 to 12
- values: bfloat16 [2048, 16, 128], P('seq', 'head'), may hold values from -6 to 6
- log_forget: float32 [16, 2048], P('head', 'seq'), may hold values from -1.6 to 0
- strength: float32 [16, 2048], P('head', 'seq'), may hold values from 0.05 to 1
- out_weight: bfloat16 [2048, 2048], P('head'), may hold values from -0.125 to 0.125
Outputs:
- mixed: bfloat16 [2048, 2048], P(('seq', 'head'))
The draws below stay inside these ranges and needn't reach their ends.
All inputs are finite; a program needn't handle non-finite values.
Results may differ from the reference program's by a relative error of at most 0.018.
Values may be sent and summed in bfloat16 or wider, within the bound.
A program may use at most 64 MiB of HBM per device.

```python
import math
import jax
import jax.numpy as jnp
from jax import lax

D = 2048
HEADS = 16
E = 128
WINDOW = 1024
CG_STEPS = 6
SEQUENCE_TOKENS = 2048


def paired(key):
    drawn_keys = jnp.clip(jax.random.normal(jax.random.fold_in(key, 101), (SEQUENCE_TOKENS, HEADS, E), jnp.float32), -6.0, 6.0)
    drawn_queries = jnp.clip(jax.random.normal(jax.random.fold_in(key, 102), (SEQUENCE_TOKENS, HEADS, E), jnp.float32), -6.0, 6.0)
    return (drawn_queries, drawn_keys)


def draw_queries(key, part):
    return paired(key)[0].astype(jnp.bfloat16)


def draw_keys(key, part):
    return paired(key)[1].astype(jnp.bfloat16)


def draw_log_forget(key, part):
    fast = jax.random.randint(jax.random.fold_in(key, 201), (HEADS,), 0, 2) == 1
    fast_rate = 1.0 / 40.0 * jnp.exp(jax.random.uniform(jax.random.fold_in(key, 202), (HEADS,), jnp.float32, -0.29, 0.29))
    slow_rate = 0.25 / SEQUENCE_TOKENS * jnp.exp(jax.random.uniform(jax.random.fold_in(key, 203), (HEADS,), jnp.float32, -0.7, 0.7))
    learning_rate = jnp.where(fast, fast_rate, slow_rate)[:, None]
    coarse_estimate = jax.random.uniform(jax.random.fold_in(key, 204), (HEADS, SEQUENCE_TOKENS), jnp.float32, 0.5, 1.5)
    table = jnp.exp(jax.random.uniform(jax.random.fold_in(key, 205), (SEQUENCE_TOKENS // 64 + 1,), jnp.float32, -0.7, 0.7))
    block_multiplier = table[jnp.arange(SEQUENCE_TOKENS) // 64]
    spike_position = jax.random.randint(jax.random.fold_in(key, 206), (2,), 0, SEQUENCE_TOKENS)
    training_loss = jax.random.uniform(jax.random.fold_in(key, 207), (HEADS, 2), jnp.float32, 0.2, 0.5)
    match_count = (jnp.arange(SEQUENCE_TOKENS)[None, :] == spike_position[:, None]).astype(jnp.float32)
    spike_events = jnp.dot(jnp.log1p(-training_loss), match_count)
    return -learning_rate * coarse_estimate * block_multiplier[None, :] + spike_events


def shard_levels(key, dims, pieces, least, high):
    level = 1.0
    for dim, shards_of in pieces:
        draws = jax.random.uniform(jax.random.fold_in(jax.random.fold_in(key, 6), dim), (shards_of,), jnp.float32, least / len(pieces), high / len(pieces))
        level = level * jnp.repeat(jnp.exp(draws), dims[dim] // shards_of).reshape((-1,) + (1,) * (len(dims) - 1 - dim))
    return level


def centred(key, extent, scale, bound, pieces=(), kind=jnp.bfloat16):
    factor_of = shard_levels(key, extent, pieces, -0.22, 0.18) if pieces else 1.0
    result = jax.random.normal(key, extent, jnp.float32) * scale * factor_of
    return jnp.minimum(jnp.maximum(result, -bound), bound).astype(kind)


def setup_inputs(seed: int = 0) -> dict:
    key_of = jax.random.split(jax.random.key(seed), 7)
    return {
        "queries": draw_queries(jax.random.fold_in(key_of[6], 71), 0),
        "keys": draw_keys(jax.random.fold_in(key_of[6], 71), 0),
        "values": centred(key_of[2], (SEQUENCE_TOKENS, HEADS, E), 1.0, 6.0, ((0, 8), (1, 4))),
        "log_forget": draw_log_forget(jax.random.fold_in(key_of[6], 71), 0),
        "strength": jnp.clip(jnp.exp(math.log(1.0) - 2.9957323 * jax.random.uniform(key_of[4], (HEADS, SEQUENCE_TOKENS), jnp.float32) ** shard_levels(key_of[4], (HEADS, SEQUENCE_TOKENS), ((0, 4), (1, 8)), -0.2, 0.2)), 0.05, 1.0),
        "out_weight": centred(key_of[5], (HEADS * E, D), (HEADS * E) ** -0.5, 0.125, ((0, 4),)),
    }


ridge = 0.25
highest = lax.Precision.HIGHEST
tiny_floor = 1e-30

def window_attention(query_rows, key_rows, value_rows, offset):
    count = query_rows.shape[0]
    block = min(512, count)
    reach = WINDOW + block
    scale = query_rows.shape[2] ** (-0.5)
    results = []
    for block_start in range(0, count, block):
        query_block = query_rows[block_start:block_start + block].astype(jnp.float32)
        key_block = key_rows[block_start:block_start + reach].astype(jnp.float32)
        value_block = value_rows[block_start:block_start + reach].astype(jnp.float32)
        query_pos = block_start + jnp.arange(block)
        key_pos = block_start - WINDOW + jnp.arange(reach)
        admitted = (key_pos[None, :] <= query_pos[:, None]) & (key_pos[None, :] > query_pos[:, None] - WINDOW) & (key_pos[None, :] + offset >= 0)
        scores = jnp.einsum('qhe,khe->hqk', query_block, key_block, precision=highest) * scale
        scores = jnp.where(admitted[None], scores, -jnp.inf)
        largest = lax.optimization_barrier(jnp.max(scores, axis=-1, keepdims=True))
        expo = jnp.exp(scores - largest)
        weights = (expo / lax.optimization_barrier(jnp.sum(expo, axis=-1, keepdims=True))).astype(jnp.bfloat16)
        results.append(jnp.einsum('hqk,khe->qhe', weights.astype(jnp.float32), value_block, precision=highest))
    return jnp.concatenate(results, axis=0)

def group_step(state, inputs):
    key_state, value_state = state
    query_part, key_part, value_part, forget_part, strength_part = inputs
    decay_sum = jnp.cumsum(forget_part, axis=1)
    length = forget_part.shape[1]
    order = jnp.arange(length)
    causal = (order[:, None] >= order[None, :])[None]
    gap = jnp.where(causal, decay_sum[:, :, None] - decay_sum[:, None, :], 0.0)
    mixing = jnp.where(causal, jnp.exp(gap), 0.0) * strength_part[:, None, :]
    leading = jnp.exp(decay_sum)[:, :, None]

    def operator(vector):
        correlation = jnp.einsum('htf,hsf->hts', vector, key_part, precision=highest)
        carried = jnp.einsum('htf,hef->hte', vector, key_state, precision=highest)
        inside = jnp.einsum('hts,hse->hte', mixing * correlation, key_part, precision=highest)
        return leading * carried + inside + ridge * vector
    solution = jnp.zeros_like(query_part)
    residual = query_part
    direction = query_part
    norm_now = lax.optimization_barrier(jnp.sum(residual * residual, axis=-1, keepdims=True))
    for iteration in range(CG_STEPS):
        image = operator(direction)
        alpha = norm_now / jnp.maximum(lax.optimization_barrier(jnp.sum(direction * image, axis=-1, keepdims=True)), tiny_floor)
        solution = solution + alpha * direction
        residual = residual - alpha * image
        norm_next = lax.optimization_barrier(jnp.sum(residual * residual, axis=-1, keepdims=True))
        direction = residual + norm_next / jnp.maximum(norm_now, tiny_floor) * direction
        norm_now = norm_next
    correlation = jnp.einsum('htf,hsf->hts', solution, key_part, precision=highest)
    output = leading * jnp.einsum('htf,hef->hte', solution, value_state, precision=highest)
    output = output + jnp.einsum('hts,hse->hte', mixing * correlation, value_part, precision=highest)
    tail = jnp.exp(decay_sum[:, -1:] - decay_sum) * strength_part
    end_factor = jnp.exp(decay_sum[:, -1])[:, None, None]
    key_state = end_factor * key_state + jnp.einsum('hse,hsf->hef', tail[:, :, None] * key_part, key_part, precision=highest)
    value_state = end_factor * value_state + jnp.einsum('hse,hsf->hef', tail[:, :, None] * value_part, key_part, precision=highest)
    return ((key_state, value_state), output)

def normalized(rows):
    wide = rows.astype(jnp.float32)
    return wide * lax.rsqrt(lax.optimization_barrier(jnp.sum(wide * wide, axis=-1, keepdims=True)) + 1e-06)

def mesa_heads(query_rows, key_rows, value_rows, log_forget, strength, key_start, value_start):
    heads_here, count, width = query_rows.shape
    group = min(256, count)
    blocks = count // group

    def blocked(array):
        shaped = array.reshape((heads_here, blocks, group) + array.shape[2:])
        return jnp.moveaxis(shaped, 1, 0)
    inputs = (blocked(query_rows), blocked(key_rows), blocked(value_rows), blocked(log_forget), blocked(strength))
    final, outputs = lax.scan(group_step, (key_start, value_start), inputs)
    return jnp.moveaxis(outputs, 0, 1).reshape(heads_here, count, width)

def reference(queries, keys, values, log_forget, strength, out_weight):
    padding = jnp.zeros((WINDOW, HEADS, E), jnp.bfloat16)
    attended = window_attention(queries, jnp.concatenate((padding, keys), 0), jnp.concatenate((padding, values), 0), 0)
    query_norm = jnp.transpose(normalized(queries), (1, 0, 2))
    key_norm = jnp.transpose(normalized(keys), (1, 0, 2))
    value_wide = jnp.transpose(values.astype(jnp.float32), (1, 0, 2))
    empty = jnp.zeros((HEADS, E, E), jnp.float32)
    mesa = mesa_heads(query_norm, key_norm, value_wide, log_forget, strength, empty, empty)
    head_out = (attended + jnp.transpose(mesa, (1, 0, 2))).astype(jnp.bfloat16)
    flat = head_out.reshape(SEQUENCE_TOKENS, HEADS * E)
    return jnp.dot(flat, out_weight, preferred_element_type=jnp.float32).astype(jnp.bfloat16)
```

```python
import functools

import jax
import jax.numpy as jnp
from jax import lax
from jax.experimental import pallas as pl
from jax.experimental.pallas import tpu as pltpu
from jax.sharding import PartitionSpec as P

WINDOW = 1024
CG_STEPS = 6
RIDGE = 0.25
TINY = 1e-30
LOW = -1e30
LOG2E = 1.4426950408889634
MESH = pl.DeviceIdType.MESH
F32 = jnp.float32
BF16 = jnp.bfloat16
K, V, Q = 0, 1, 2


def dot(a, b):
    return lax.dot_general(a, b, (((1,), (0,)), ((), ())), preferred_element_type=F32)


def dot_t(a, b):
    return lax.dot_general(a, b, (((1,), (1,)), ((), ())), preferred_element_type=F32)


def dot_tl(a, b):
    return lax.dot_general(a, b, (((0,), (0,)), ((), ())), preferred_element_type=F32)


def kernel(
    n, nz, back,
    q_hbm, k_hbm, v_hbm, f_ref, s_ref, w_hbm, out_ref,
    raw, wide, own, fs_own, kv, qb, fs, st, stl, w, mix, wgt, wk, sk, sv, sacc, xs, rs, ds, nrm, att, am, al,
    hout, hother, prt, rsend, lsend, rrecv, lrecv,
    in_s, w_sem, kv_s, kv_r, sib_s, q_r, fs_s, fs_r, st_s, st_r, rl_s, h_sem, rs_s, rs_r, ls_s, ls_r,
):
    me = lax.axis_index("seq")
    z = lax.axis_index("head")
    chip, core = me // 2, me % 2
    sib = chip * 2 + (1 - core)
    chips = n // 2
    window = 2 * back
    half, tok, width = kv.shape[2], kv.shape[3], kv.shape[4]
    heads = 2 * half
    chains = 2 * half
    far_max = max(n - 2 * (back + 1), 0)
    relay = chips == 4 and back == 2

    loads = [pltpu.make_async_copy(ref, raw.at[i], in_s.at[i]) for i, ref in ((K, k_hbm), (V, v_hbm), (Q, q_hbm))]
    for i in (K, Q, V):
        loads[i].start()
    w_copy = pltpu.make_async_copy(w_hbm, w, w_sem)
    w_copy.start()

    barrier = pltpu.get_barrier_semaphore()
    for k in range(1, n):
        pl.semaphore_signal(barrier, inc=1, device_id=((me + k) % n, z), device_id_type=MESH)
    for k in range(1, nz):
        pl.semaphore_signal(barrier, inc=1, device_id=(me, (z + k) % nz), device_id_type=MESH)

    def spread(i):
        loads[i].wait()
        wide[i] = raw[i].astype(F32)
        for g in range(2):
            for h in range(half):
                own[i, g, h] = wide[i, pl.ds(g * half + h, tok, stride=heads), :].astype(BF16)

    for g in range(2):
        fs_own[g, :half] = f_ref[g * half:(g + 1) * half, :]
        fs_own[g, half:] = s_ref[g * half:(g + 1) * half, :]
    spread(K)
    pl.semaphore_wait(barrier, n - 1 + nz - 1)

    def remote(src, dst, s_sem, r_sem, s, h):
        return pltpu.make_async_remote_copy(
            src_ref=src, dst_ref=dst, send_sem=s_sem, recv_sem=r_sem,
            device_id=(s, h), device_id_type=MESH)

    def halo_copy(d, g, part, h):
        return remote(own.at[part, g, h], kv.at[window - 2 * d + core, part, h], kv_s.at[d - 1, g, part, h],
                      kv_r.at[window - 2 * d + core, part, h], (chip + d) * 2 + g, z)

    def straight(part, h):
        return part == V and h == half - 1

    def halo_each(part, act):
        for h in range(half):
            for d in range(back, 0, -1):
                ok = chip + d < chips
                if relay and d == 1:
                    ok = ok & ((chip != 1) | (core == 1)) if straight(part, h) else ok & (chip != 1)

                @pl.when(ok)
                def _():
                    for g in range(2):
                        act(halo_copy(d, g, part, h))

    def relay_copy(g, part, h):
        return remote(kv.at[g, part, h], kv.at[window - 2 + g, part, h], rl_s.at[g, part, h],
                      kv_r.at[window - 2 + g, part, h], me - 2, z)

    def relayed(part, h):
        return [0] if straight(part, h) else [0, 1]

    def await_kv(slot, part, h):
        remote(own.at[0, 0, 0], kv.at[slot, part, h], kv_s.at[0, 0, 0, 0], kv_r.at[slot, part, h], me, z).wait_recv()

    def sib_copy(part):
        other = 1 - core
        if part == Q:
            return remote(own.at[Q, other], qb.at[core], sib_s.at[Q], q_r, sib, z)
        return remote(own.at[part, other], kv.at[window + core, part], sib_s.at[part], sib_r(part, core), sib, z)

    def sib_r(part, c):
        return kv_r.at[window + c, part, 0]

    def fs_copy(j, owner):
        return remote(fs_own.at[j % 2], fs.at[owner], fs_s.at[j], fs_r.at[owner], j, z)

    sib_copy(K).start()
    for j in range(n):
        @pl.when((j // 2 >= chip) & (j != me))
        def _():
            fs_copy(j, me).start()
    halo_each(K, lambda c: c.start())
    spread(Q)
    sib_copy(Q).start()
    spread(V)
    sib_copy(V).start()

    row = lax.broadcasted_iota(jnp.int32, (tok, tok), 0)
    col = lax.broadcasted_iota(jnp.int32, (tok, tok), 1)
    tri = row >= col
    eye = row == col

    def to_col(r):
        return jnp.sum(jnp.where(eye, jnp.broadcast_to(r, (tok, tok)), 0.0), axis=1, keepdims=True)

    def to_row(c):
        return jnp.sum(jnp.where(eye, jnp.broadcast_to(c, (tok, tok)), 0.0), axis=0, keepdims=True)

    def sums_col(r):
        return jnp.sum(jnp.where(tri, jnp.broadcast_to(r, (tok, tok)), 0.0), axis=1, keepdims=True)

    def inv_norm(x):
        x = x.astype(F32)
        return lax.rsqrt(jnp.sum(x * x, axis=-1, keepdims=True) + 1e-6)

    def tail_of(f, s):
        return jnp.exp(jnp.sum(f, axis=1, keepdims=True) - sums_col(f)) * to_col(s)

    def decay(f):
        return jnp.exp(jnp.sum(f, axis=1, keepdims=True))

    def local_state(g, h, parts):
        k = own[K, g, h]
        r = inv_norm(k)
        scaled = (tail_of(fs_own[g, h:h + 1, :], fs_own[g, half + h:half + h + 1, :]) * r) * k.astype(F32)
        if K in parts:
            stl[g, K, h] = dot_tl((scaled * r).astype(BF16), k).astype(BF16)
        if V in parts:
            stl[g, V, h] = dot_tl(scaled.astype(BF16), own[V, g, h]).astype(BF16)

    def st_copy(j, owner):
        return remote(stl.at[j % 2], st.at[owner], st_s.at[j], st_r.at[owner], j, z)

    def near_copy(j, owner):
        return remote(stl.at[j % 2, K], st.at[owner, K], st_s.at[j], st_r.at[owner], j, z)

    if relay:
        @pl.when(chip == 1)
        def _():
            for g in range(2):
                for h in range(half):
                    local_state(g, h, (K,))
                near_copy(4 + g, me).start()

    if far_max > 0:
        @pl.when(chip + back + 1 < chips)
        def _():
            for g in range(2):
                for h in range(half):
                    local_state(g, h, (K, V))
            for j in range(2 * (back + 1), n):
                @pl.when(j // 2 > chip + back)
                def _():
                    st_copy(j, me).start()

    halo_each(V, lambda c: c.start())

    kv[window + core, K] = own[K, core]
    kv[window + core, V] = own[V, core]
    qb[core] = own[Q, core]
    fs[me] = fs_own[core]

    for part in (K, Q, V):
        sib_copy(part).wait_send()
    for part in (K, V):
        remote(own.at[0, 0], kv.at[window + 1 - core, part], sib_s.at[0], sib_r(part, 1 - core), sib, z).wait_recv()
    remote(own.at[0, 0], qb.at[1 - core], sib_s.at[Q], q_r, sib, z).wait_recv()
    for j in range(n):
        @pl.when((j // 2 <= chip) & (j != me))
        def _():
            fs_copy(me, j).wait_recv()

        @pl.when((j // 2 >= chip) & (j != me))
        def _():
            fs_copy(j, me).wait_send()

    def gates(shard, h):
        at = (shard + n) % n
        both = fs[at]
        return both[h:h + 1, :], both[half + h:half + h + 1, :]

    leads = []
    for b in range(2):
        for h in range(half):
            i = b * half + h
            f, s = gates(chip * 2 + b, h)
            c_col = sums_col(f)
            c_row = to_row(c_col)
            r_row = to_row(inv_norm(kv[window + b, K, h]))
            mix[i] = jnp.where(tri, jnp.exp(jnp.minimum(c_col - c_row, 0.0)), 0.0) * (s * r_row * r_row)
            nrm[i] = jnp.broadcast_to(1.0 / r_row, (8, tok))
            q = qb[b, h].astype(F32)
            ds[i] = q * lax.rsqrt(jnp.sum(q * q, axis=-1, keepdims=True) + 1e-6)
            rs[i] = ds[i]
            xs[i] = jnp.zeros((tok, width), F32)
            leads.append(jnp.exp(c_col))

    for h in range(half):
        later = 1.0
        for j in range(window, -1, -1):
            ok = chip * 2 + j >= window
            f, s = gates(chip * 2 - window + j, h)
            part = tail_of(f, s)
            if j < window:
                part = jnp.where(ok, part * later, 0.0)
                later = jnp.where(ok, later * decay(f), 1.0)
            wgt[h, j] = jnp.broadcast_to(part, (tok, width))
        nrm_far = later
        wgt_far = jnp.broadcast_to(nrm_far, (1, width))
        sacc[2, h, 0:1] = wgt_far

    unit = width ** (-0.5) * LOG2E

    def attend(b, h, slots, first):
        i = b * half + h
        q = qb[b, h]
        parts = []
        for slot in slots:
            sc = dot_t(q, kv[slot, K, h])
            ok = chip * 2 + slot >= window
            if slot == b:
                sc = jnp.where((col > row) & ok, sc, LOW)
            elif slot == b + window:
                sc = jnp.where(tri, sc, LOW)
            elif slot < window:
                sc = jnp.where(ok, sc, LOW)
            parts.append(sc)
        top = jnp.max(functools.reduce(jnp.maximum, parts), axis=1, keepdims=True) * unit
        if not first:
            before = am[i][:, 0:1]
            top = jnp.maximum(top, before)
        total = acc = None
        for slot, sc in zip(slots, parts):
            e = jnp.exp2(sc * unit - top)
            total = e if total is None else total + e
            pv = dot(e.astype(BF16), kv[slot, V, h])
            acc = pv if acc is None else acc + pv
        total = jnp.sum(total, axis=1, keepdims=True)
        if not first:
            shrink = jnp.exp2(before - top)
            total = total + shrink * al[i][:, 0:1]
            acc = acc + shrink * att[i]
        am[i] = jnp.broadcast_to(top, (tok, width))
        al[i] = jnp.broadcast_to(total, (tok, width))
        att[i] = acc

    for h in range(half):
        attend(0, h, [window], True)
        attend(1, h, [window, window + 1], True)

    def weighted(j, h, accumulate):
        k = kv[j, K, h]
        r = inv_norm(k)
        scaled = (wgt[h, j] * r) * k.astype(F32)
        wk[h, j] = scaled.astype(BF16)
        if accumulate:
            sacc[K, h] = sacc[K, h] + dot_tl((scaled * r).astype(BF16), k)

    def begin(part):
        for h in range(half):
            acc = jnp.zeros((width, width), F32)
            for j in range(far_max):
                ok = j // 2 < chip - back
                f, s = gates(j, h)
                acc = jnp.where(ok, decay(f) * acc + st[j, part, h].astype(F32), acc)
            sacc[part, h] = sacc[2, h, 0:1] * acc

    def finish(part, out):
        for h in range(half):
            f, s = gates(chip * 2, h)
            out[h] = sacc[part, h].astype(BF16)
            if part == K:
                k = kv[window, K, h]
                r = inv_norm(k)
                scaled = (wgt[h, window] * r) * k.astype(F32)
                new = dot_tl((scaled * r).astype(BF16), k)
                wk[h, window] = scaled.astype(BF16)
            else:
                new = dot_tl(wk[h, window], kv[window, V, h])
            out[half + h] = (decay(f) * sacc[part, h] + new).astype(BF16)

    def arrive(part, d, h):
        for g in range(2):
            slot = window - 2 * d + g

            @pl.when(chip >= d)
            def _():
                await_kv(slot, part, h)

            @pl.when(chip < d)
            def _():
                kv[slot, part, h] = jnp.zeros((tok, width), BF16)

    def pass_on(part, h):
        if relay:
            @pl.when(chip == 3)
            def _():
                for g in relayed(part, h):
                    relay_copy(g, part, h).start()

    for j in range(far_max):
        @pl.when(j // 2 < chip - back)
        def _():
            remote(stl.at[0], st.at[j], st_s.at[0], st_r.at[j], me, z).wait_recv()
    begin(K)
    for d in range(back, 0, -1):
        late = relay and d == 1

        def near(accumulate):
            for h in range(half):
                arrive(K, d, h)
                if d == back:
                    pass_on(K, h)
                for g in range(2):
                    weighted(window - 2 * d + g, h, accumulate)

        if late:
            @pl.when(chip != 2)
            def _():
                near(True)

            @pl.when(chip == 2)
            def _():
                for j in (2, 3):
                    remote(stl.at[0, K], st.at[j, K], st_s.at[0], st_r.at[j], me, z).wait_recv()
                for h in range(half):
                    f, s = gates(3, h)
                    sacc[K, h] = sacc[K, h] + decay(f) * st[2, K, h].astype(F32) + st[3, K, h].astype(F32)
        else:
            near(True)
    finish(K, sk)

    def step(_, carry):
        norms = []
        for i in range(chains):
            b, h = divmod(i, half)
            now = carry[i]
            dirn = ds[i]
            low = dirn.astype(BF16)
            k = kv[window + b, K, h]
            p = (mix[i] * dot_t(low, k)).astype(BF16)
            image = leads[i] * dot(low, sk[i]) + dot(p, k) + RIDGE * dirn
            alpha = now / jnp.maximum(jnp.sum(dirn * image, axis=-1, keepdims=True), TINY)
            xs[i] = xs[i] + alpha * dirn
            res = rs[i] - alpha * image
            rs[i] = res
            new = jnp.sum(res * res, axis=-1, keepdims=True)
            ds[i] = res + (new / jnp.maximum(now, TINY)) * dirn
            norms.append(new)
        return tuple(norms)

    start = tuple(jnp.sum(ds[i] * ds[i], axis=-1, keepdims=True) for i in range(chains))
    mid = CG_STEPS // 2
    norms = lax.fori_loop(0, mid, step, start)
    for h in range(half - 1):
        arrive(V, back, h)
        pass_on(V, h)
    lax.fori_loop(mid, CG_STEPS, step, norms)

    arrive(V, back, half - 1)
    pass_on(V, half - 1)
    begin(V)
    for d in range(back, 0, -1):
        if d < back:
            for h in range(half):
                arrive(V, d, h)
        if relay and d == 1:
            @pl.when(chip == 2)
            def _():
                for h in range(half):
                    arrive(K, 1, h)
                    for g in range(2):
                        weighted(window - 2 + g, h, False)
        near_slots = [window - 2 * d, window - 2 * d + 1]
        for h in range(half):
            sacc[V, h] = sacc[V, h] + sum(dot_tl(wk[h, j], kv[j, V, h]) for j in near_slots)
            for b in range(2):
                attend(b, h, [j for j in near_slots if j >= b], False)
    finish(V, sv)

    for b in range(2):
        for h in range(half):
            i = b * half + h
            low = xs[i].astype(BF16)
            p = ((mix[i] * nrm[i][0:1, :]) * dot_t(low, kv[window + b, K, h])).astype(BF16)
            mesa = leads[i] * dot(low, sv[i]) + dot(p, kv[window + b, V, h])
            hout[b, :, h * width:(h + 1) * width] = (att[i] / al[i] + mesa).astype(BF16)

    swap = remote(hout.at[1 - core], hother, h_sem.at[0], h_sem.at[1], sib, z)
    swap.start()
    w_copy.wait()
    prt[...] = dot(hout[core], w[core])
    swap.wait()

    chunk = tok // nz
    pieces = rsend.shape[1]
    cols = w.shape[2] // pieces

    def at(p):
        return pl.ds(pl.multiple_of(p * cols, cols), cols)

    prt[...] += dot(hother[...], w[1 - core])

    def partial(d, p):
        return prt[d * chunk:(d + 1) * chunk, at(p)]

    def right(d, p):
        return remote(rsend.at[d, p], rrecv.at[d, p], rs_s.at[d, p], rs_r.at[d, p], me, (z + 1) % nz)

    def left(d, p):
        return remote(lsend.at[d, p], lrecv.at[d, p], ls_s.at[d, p], ls_r.at[d, p], me, (z + nz - 1) % nz)

    def go_right(d):
        @pl.when(z < d)
        def _():
            @pl.loop(0, pieces)
            def _(p):
                @pl.when(z == 0)
                def _():
                    rsend[d, p] = partial(d, p).astype(BF16)

                @pl.when(z > 0)
                def _():
                    right(d, p).wait_recv()
                    rsend[d, p] = (partial(d, p) + rrecv[d, p].astype(F32)).astype(BF16)

                right(d, p).start()

    def go_left(d):
        @pl.when(z > d)
        def _():
            @pl.loop(0, pieces)
            def _(p):
                @pl.when(z == nz - 1)
                def _():
                    lsend[d, p] = partial(d, p).astype(BF16)

                @pl.when(z < nz - 1)
                def _():
                    left(d, p).wait_recv()
                    lsend[d, p] = (partial(d, p) + lrecv[d, p].astype(F32)).astype(BF16)

                left(d, p).start()

    @pl.when(z < nz // 2)
    def _():
        for k in range(nz - 1):
            go_right(nz - 1 - k)
            go_left(k)

    @pl.when(z >= nz // 2)
    def _():
        for k in range(nz - 1):
            go_left(k)
            go_right(nz - 1 - k)

    for d in range(nz):
        @pl.when(z == d)
        def _():
            @pl.loop(0, pieces)
            def _(p):
                total = partial(d, p)
                if d > 0:
                    right(d, p).wait_recv()
                    total = total + rrecv[d, p].astype(F32)
                if d < nz - 1:
                    left(d, p).wait_recv()
                    total = total + lrecv[d, p].astype(F32)
                out_ref[:, at(p)] = total.astype(BF16)

    for d in range(nz):
        for p in range(pieces):
            @pl.when(z < d)
            def _():
                right(d, p).wait_send()

            @pl.when(z > d)
            def _():
                left(d, p).wait_send()

    halo_each(K, lambda c: c.wait_send())
    halo_each(V, lambda c: c.wait_send())
    if relay:
        @pl.when(chip == 3)
        def _():
            for part in (K, V):
                for h in range(half):
                    for g in relayed(part, h):
                        relay_copy(g, part, h).wait_send()

        @pl.when(chip == 1)
        def _():
            for g in range(2):
                near_copy(4 + g, me).wait_send()
    if far_max > 0:
        for j in range(2 * (back + 1), n):
            @pl.when(j // 2 > chip + back)
            def _():
                st_copy(j, me).wait_send()


def on_device(queries, keys, values, log_forget, strength, out_weight):
    tok, heads, width = queries.shape
    n, nz = lax.axis_size("seq"), lax.axis_size("head")
    half = heads // 2
    back = max(WINDOW // (2 * tok), 1)
    flat = [x.reshape(tok * heads, width) for x in (queries, keys, values)]
    model = out_weight.shape[1]
    weight = out_weight.reshape(2, half * width, model)
    chunk = tok // nz
    slots = 2 * back + 2
    chains = 2 * half
    pieces = 4
    held = max(n - 2 * (back + 1), 4)
    dma = pltpu.SemaphoreType.DMA
    vmem = pl.BlockSpec(memory_space=pltpu.VMEM)
    hbm = pl.BlockSpec(memory_space=pl.ANY)
    return pl.pallas_call(
        functools.partial(kernel, n, nz, back),
        out_shape=jax.ShapeDtypeStruct((chunk, model), BF16),
        in_specs=[hbm, hbm, hbm, vmem, vmem, hbm],
        out_specs=vmem,
        scratch_shapes=[
            pltpu.VMEM((3, tok * heads, width), BF16),
            pltpu.VMEM((3, tok * heads, width), F32),
            pltpu.VMEM((3, 2, half, tok, width), BF16),
            pltpu.VMEM((2, 2 * half, tok), F32),
            pltpu.VMEM((slots, 2, half, tok, width), BF16),
            pltpu.VMEM((2, half, tok, width), BF16),
            pltpu.VMEM((n, 2 * half, tok), F32),
            pltpu.VMEM((held, 2, half, width, width), BF16),
            pltpu.VMEM((2, 2, half, width, width), BF16),
            pltpu.VMEM((2, half * width, model), BF16),
            pltpu.VMEM((chains, tok, tok), F32),
            pltpu.VMEM((half, slots - 1, tok, width), F32),
            pltpu.VMEM((half, slots - 1, tok, width), BF16),
            pltpu.VMEM((chains, width, width), BF16),
            pltpu.VMEM((chains, width, width), BF16),
            pltpu.VMEM((3, half, width, width), F32),
            pltpu.VMEM((chains, tok, width), F32),
            pltpu.VMEM((chains, tok, width), F32),
            pltpu.VMEM((chains, tok, width), F32),
            pltpu.VMEM((chains, 8, tok), F32),
            pltpu.VMEM((chains, tok, width), F32),
            pltpu.VMEM((chains, tok, width), F32),
            pltpu.VMEM((chains, tok, width), F32),
            pltpu.VMEM((2, tok, half * width), BF16),
            pltpu.VMEM((tok, half * width), BF16),
            pltpu.VMEM((tok, model), F32),
            pltpu.VMEM((nz, pieces, chunk, model // pieces), BF16),
            pltpu.VMEM((nz, pieces, chunk, model // pieces), BF16),
            pltpu.VMEM((nz, pieces, chunk, model // pieces), BF16),
            pltpu.VMEM((nz, pieces, chunk, model // pieces), BF16),
            dma((3,)), dma(()),
            dma((back, 2, 2, half)), dma((slots, 2, half)), dma((3,)), dma(()), dma((n,)), dma((n,)),
            dma((n,)), dma((n,)), dma((2, 2, half)), dma((2,)),
            dma((nz, pieces)), dma((nz, pieces)), dma((nz, pieces)), dma((nz, pieces)),
        ],
        compiler_params=pltpu.CompilerParams(
            collective_id=0, has_side_effects=True, vmem_limit_bytes=56 * 1024 * 1024),
    )(*flat, log_forget, strength, weight)


def solution(mesh):
    in_specs = (
        P("seq", "head", None),
        P("seq", "head", None),
        P("seq", "head", None),
        P("head", "seq"),
        P("head", "seq"),
        P("head", None),
    )
    return jax.shard_map(
        on_device, mesh=mesh, in_specs=in_specs, out_specs=P(("seq", "head"), None), check_vma=False)
```

```python
import functools

import jax
import jax.numpy as jnp
from jax import lax
from jax.experimental import pallas as pl
from jax.experimental.pallas import tpu as pltpu
from jax.sharding import PartitionSpec as P

WINDOW = 1024
CG_STEPS = 6
RIDGE = 0.25
TINY = 1e-30
LOW = -1e30
LOG2E = 1.4426950408889634
MESH = pl.DeviceIdType.MESH
F32 = jnp.float32
BF16 = jnp.bfloat16
K, V, Q = 0, 1, 2


def dot(a, b):
    return lax.dot_general(a, b, (((1,), (0,)), ((), ())), preferred_element_type=F32)


def dot_t(a, b):
    return lax.dot_general(a, b, (((1,), (1,)), ((), ())), preferred_element_type=F32)


def dot_tl(a, b):
    return lax.dot_general(a, b, (((0,), (0,)), ((), ())), preferred_element_type=F32)


def kernel(
    n, nz, back,
    q_hbm, k_hbm, v_hbm, f_ref, s_ref, w_hbm, out_ref,
    raw, wide, own, fs_own, kv, qb, fs, st, stl, w, mix, wgt, wk, own_st, sk, sv, sacc, xs, rs, ds, nrm, att, am, al,
    hout, hother, prt, rsend, lsend, rrecv, lrecv,
    in_s, w_sem, kv_s, kv_r, sib_s, q_r, fs_s, fs_r, st_s, st_r, rl_s, h_sem, rs_s, rs_r, ls_s, ls_r,
):
    me = lax.axis_index("seq")
    z = lax.axis_index("head")
    chip, core = me // 2, me % 2
    sib = chip * 2 + (1 - core)
    chips = n // 2
    window = 2 * back
    half, tok, width = kv.shape[2], kv.shape[3], kv.shape[4]
    heads = 2 * half
    chains = 2 * half
    far_max = max(n - 2 * (back + 1), 0)
    relay = chips == 4 and back == 2

    loads = [pltpu.make_async_copy(ref, raw.at[i], in_s.at[i]) for i, ref in ((K, k_hbm), (V, v_hbm), (Q, q_hbm))]
    for i in (K, Q, V):
        loads[i].start()
    w_copy = pltpu.make_async_copy(w_hbm, w, w_sem)
    w_copy.start()

    barrier = pltpu.get_barrier_semaphore()
    for k in range(1, n):
        pl.semaphore_signal(barrier, inc=1, device_id=((me + k) % n, z), device_id_type=MESH)
    for k in range(1, nz):
        pl.semaphore_signal(barrier, inc=1, device_id=(me, (z + k) % nz), device_id_type=MESH)

    def spread(i):
        loads[i].wait()
        wide[i] = raw[i].astype(F32)
        for g in range(2):
            for h in range(half):
                own[i, g, h] = wide[i, pl.ds(g * half + h, tok, stride=heads), :].astype(BF16)

    for g in range(2):
        fs_own[g, :half] = f_ref[g * half:(g + 1) * half, :]
        fs_own[g, half:] = s_ref[g * half:(g + 1) * half, :]
    spread(K)
    pl.semaphore_wait(barrier, n - 1 + nz - 1)

    def remote(src, dst, s_sem, r_sem, s, h):
        return pltpu.make_async_remote_copy(
            src_ref=src, dst_ref=dst, send_sem=s_sem, recv_sem=r_sem,
            device_id=(s, h), device_id_type=MESH)

    def halo_copy(d, g, part, h):
        return remote(own.at[part, g, h], kv.at[window - 2 * d + core, part, h], kv_s.at[d - 1, g, part, h],
                      kv_r.at[window - 2 * d + core, part, h], (chip + d) * 2 + g, z)

    def straight(part, h):
        return part == V and h == half - 1

    def halo_each(part, act):
        for h in range(half):
            for d in range(back, 0, -1):
                ok = chip + d < chips
                if relay and d == 1:
                    ok = ok & ((chip != 1) | (core == 1)) if straight(part, h) else ok & (chip != 1)

                @pl.when(ok)
                def _():
                    for g in range(2):
                        act(halo_copy(d, g, part, h))

    def relay_copy(g, part, h):
        return remote(kv.at[g, part, h], kv.at[window - 2 + g, part, h], rl_s.at[g, part, h],
                      kv_r.at[window - 2 + g, part, h], me - 2, z)

    def relayed(part, h):
        return [0] if straight(part, h) else [0, 1]

    def await_kv(slot, part, h):
        remote(own.at[0, 0, 0], kv.at[slot, part, h], kv_s.at[0, 0, 0, 0], kv_r.at[slot, part, h], me, z).wait_recv()

    def sib_copy(part):
        other = 1 - core
        if part == Q:
            return remote(own.at[Q, other], qb.at[core], sib_s.at[Q], q_r, sib, z)
        return remote(own.at[part, other], kv.at[window + core, part], sib_s.at[part], sib_r(part, core), sib, z)

    def sib_r(part, c):
        return kv_r.at[window + c, part, 0]

    def fs_copy(j, owner):
        return remote(fs_own.at[j % 2], fs.at[owner], fs_s.at[j], fs_r.at[owner], j, z)

    sib_copy(K).start()
    for j in range(n):
        @pl.when((j // 2 >= chip) & (j != me))
        def _():
            fs_copy(j, me).start()
    halo_each(K, lambda c: c.start())
    spread(Q)
    sib_copy(Q).start()
    spread(V)
    sib_copy(V).start()

    row = lax.broadcasted_iota(jnp.int32, (tok, tok), 0)
    col = lax.broadcasted_iota(jnp.int32, (tok, tok), 1)
    tri = row >= col
    eye = row == col

    def to_col(r):
        return jnp.sum(jnp.where(eye, jnp.broadcast_to(r, (tok, tok)), 0.0), axis=1, keepdims=True)

    def to_row(c):
        return jnp.sum(jnp.where(eye, jnp.broadcast_to(c, (tok, tok)), 0.0), axis=0, keepdims=True)

    def sums_col(r):
        return jnp.sum(jnp.where(tri, jnp.broadcast_to(r, (tok, tok)), 0.0), axis=1, keepdims=True)

    def inv_norm(x):
        x = x.astype(F32)
        return lax.rsqrt(jnp.sum(x * x, axis=-1, keepdims=True) + 1e-6)

    def tail_of(f, s):
        return jnp.exp(jnp.sum(f, axis=1, keepdims=True) - sums_col(f)) * to_col(s)

    def decay(f):
        return jnp.exp(jnp.sum(f, axis=1, keepdims=True))

    kv[window + core, K] = own[K, core]
    kv[window + core, V] = own[V, core]
    qb[core] = own[Q, core]
    fs[me] = fs_own[core]

    def sib_wait(part):
        sib_copy(part).wait_send()
        dst = qb.at[1 - core] if part == Q else kv.at[window + 1 - core, part]
        remote(own.at[0, 0], dst, sib_s.at[0], q_r if part == Q else sib_r(part, 1 - core), sib, z).wait_recv()

    sib_wait(K)
    for j in range(n):
        @pl.when((j // 2 <= chip) & (j != me))
        def _():
            fs_copy(me, j).wait_recv()

        @pl.when((j // 2 >= chip) & (j != me))
        def _():
            fs_copy(j, me).wait_send()

    def gates(shard, h):
        at = (shard + n) % n
        both = fs[at]
        return both[h:h + 1, :], both[half + h:half + h + 1, :]

    def st_copy(part, to, owner):
        return remote(stl.at[part], st.at[owner, part], st_s.at[part, to], st_r.at[part, owner], to * 2 + core, z)

    def await_st(part, owner):
        remote(stl.at[part], st.at[owner, part], st_s.at[part, 0], st_r.at[part, owner], me, z).wait_recv()

    def st_each(part, act):
        for to in range(1, chips):
            ok = to > chip + back
            if relay and part == K and to == 2:
                ok = ok | (chip == 1)

            @pl.when(ok)
            def _():
                act(st_copy(part, to, chip))

    if relay:
        sends_key = chip < 2
    else:
        sends_key = chip + back + 1 < chips
    sends_val = chip + back + 1 < chips

    def lhs(j, h):
        k = kv[j, K, h]
        r = inv_norm(k)
        scaled = (wgt[h, j] * r) * k.astype(F32)
        wk[h, j] = scaled.astype(BF16)
        return (scaled * r).astype(BF16)

    for h in range(half):
        for b in range(2):
            f, s = gates(chip * 2 + b, h)
            wgt[h, window + b] = jnp.broadcast_to(tail_of(f, s), (tok, width))
        own_st[K, h] = dot_tl(lhs(window, h), kv[window, K, h])

    def send_state(part):
        for h in range(half):
            f, s = gates(chip * 2 + 1, h)
            left_side = lhs(window + 1, h) if part == K else wk[h, window + 1]
            stl[part, h] = (decay(f) * own_st[part, h] + dot_tl(left_side, kv[window + 1, part, h])).astype(BF16)
        st_each(part, lambda c: c.start())

    @pl.when(sends_key)
    def _():
        send_state(K)

    halo_each(V, lambda c: c.start())

    sib_wait(V)
    for h in range(half):
        own_st[V, h] = dot_tl(wk[h, window], kv[window, V, h])

    sib_wait(Q)
    leads = []
    for b in range(2):
        for h in range(half):
            i = b * half + h
            f, s = gates(chip * 2 + b, h)
            c_col = sums_col(f)
            c_row = to_row(c_col)
            r_row = to_row(inv_norm(kv[window + b, K, h]))
            mix[i] = jnp.where(tri, jnp.exp(jnp.minimum(c_col - c_row, 0.0)), 0.0) * (s * r_row * r_row)
            nrm[i] = jnp.broadcast_to(1.0 / r_row, (8, tok))
            q = qb[b, h].astype(F32)
            ds[i] = q * lax.rsqrt(jnp.sum(q * q, axis=-1, keepdims=True) + 1e-6)
            rs[i] = ds[i]
            xs[i] = jnp.zeros((tok, width), F32)
            leads.append(jnp.exp(c_col))

    for h in range(half):
        later = 1.0
        for j in range(window - 1, -1, -1):
            ok = chip * 2 + j >= window
            f, s = gates(chip * 2 - window + j, h)
            wgt[h, j] = jnp.broadcast_to(jnp.where(ok, tail_of(f, s) * later, 0.0), (tok, width))
            later = jnp.where(ok, later * decay(f), 1.0)
        sacc[2, h, 0:1] = jnp.broadcast_to(later, (1, width))

    unit = width ** (-0.5) * LOG2E

    def attend(b, h, slots, first):
        i = b * half + h
        q = qb[b, h]
        parts = []
        for slot in slots:
            sc = dot_t(q, kv[slot, K, h])
            ok = chip * 2 + slot >= window
            if slot == b:
                sc = jnp.where((col > row) & ok, sc, LOW)
            elif slot == b + window:
                sc = jnp.where(tri, sc, LOW)
            elif slot < window:
                sc = jnp.where(ok, sc, LOW)
            parts.append(sc)
        top = jnp.max(functools.reduce(jnp.maximum, parts), axis=1, keepdims=True) * unit
        if not first:
            before = am[i][:, 0:1]
            top = jnp.maximum(top, before)
        total = acc = None
        for slot, sc in zip(slots, parts):
            e = jnp.exp2(sc * unit - top)
            total = e if total is None else total + e
            pv = dot(e.astype(BF16), kv[slot, V, h])
            acc = pv if acc is None else acc + pv
        total = jnp.sum(total, axis=1, keepdims=True)
        if not first:
            shrink = jnp.exp2(before - top)
            total = total + shrink * al[i][:, 0:1]
            acc = acc + shrink * att[i]
        am[i] = jnp.broadcast_to(top, (tok, width))
        al[i] = jnp.broadcast_to(total, (tok, width))
        att[i] = acc

    for h in range(half):
        attend(0, h, [window], True)
        attend(1, h, [window, window + 1], True)

    def chip_decay(c, h):
        return decay(gates(c * 2, h)[0]) * decay(gates(c * 2 + 1, h)[0])

    def far_state(part, h):
        acc = jnp.zeros((width, width), F32)
        for c in range(far_max // 2):
            acc = jnp.where(c < chip - back, chip_decay(c, h) * acc + st[c, part, h].astype(F32), acc)
        return sacc[2, h, 0:1] * acc

    def await_far(part):
        for c in range(far_max // 2):
            @pl.when(c < chip - back)
            def _():
                await_st(part, c)

    def finish(part, out):
        for h in range(half):
            f, s = gates(chip * 2, h)
            acc = sacc[part, h] + far_state(part, h)
            out[h] = acc.astype(BF16)
            out[half + h] = (decay(f) * acc + own_st[part, h]).astype(BF16)

    def arrive(part, d, h):
        for g in range(2):
            slot = window - 2 * d + g

            @pl.when(chip >= d)
            def _():
                await_kv(slot, part, h)

            @pl.when(chip < d)
            def _():
                kv[slot, part, h] = jnp.zeros((tok, width), BF16)

    def pass_on(part, h):
        if relay:
            @pl.when(chip == 3)
            def _():
                for g in relayed(part, h):
                    relay_copy(g, part, h).start()

    for h in range(half):
        sacc[K, h] = jnp.zeros((width, width), F32)
    for d in range(back, 0, -1):
        late = relay and d == 1

        def near():
            for h in range(half):
                arrive(K, d, h)
                if d == back:
                    pass_on(K, h)
                for g in range(2):
                    j = window - 2 * d + g
                    sacc[K, h] = sacc[K, h] + dot_tl(lhs(j, h), kv[j, K, h])

        if late:
            @pl.when(chip != 2)
            def _():
                near()

            @pl.when(chip == 2)
            def _():
                await_st(K, 1)
                for h in range(half):
                    sacc[K, h] = sacc[K, h] + st[1, K, h].astype(F32)
        else:
            near()
    await_far(K)
    finish(K, sk)

    def step(_, carry):
        norms = []
        for i in range(chains):
            b, h = divmod(i, half)
            now = carry[i]
            dirn = ds[i]
            low = dirn.astype(BF16)
            k = kv[window + b, K, h]
            p = (mix[i] * dot_t(low, k)).astype(BF16)
            image = leads[i] * dot(low, sk[i]) + dot(p, k) + RIDGE * dirn
            alpha = now / jnp.maximum(jnp.sum(dirn * image, axis=-1, keepdims=True), TINY)
            xs[i] = xs[i] + alpha * dirn
            res = rs[i] - alpha * image
            rs[i] = res
            new = jnp.sum(res * res, axis=-1, keepdims=True)
            ds[i] = res + (new / jnp.maximum(now, TINY)) * dirn
            norms.append(new)
        return tuple(norms)

    start = tuple(jnp.sum(ds[i] * ds[i], axis=-1, keepdims=True) for i in range(chains))
    mid = CG_STEPS // 2
    norms = lax.fori_loop(0, mid, step, start)
    for h in range(half - 1):
        arrive(V, back, h)
        pass_on(V, h)
    lax.fori_loop(mid, CG_STEPS, step, norms)

    arrive(V, back, half - 1)
    pass_on(V, half - 1)
    for h in range(half):
        sacc[V, h] = jnp.zeros((width, width), F32)
    for d in range(back, 0, -1):
        if d < back:
            for h in range(half):
                arrive(V, d, h)
        if relay and d == 1:
            @pl.when(chip == 2)
            def _():
                for h in range(half):
                    arrive(K, 1, h)
                    for g in range(2):
                        lhs(window - 2 + g, h)
        near_slots = [window - 2 * d, window - 2 * d + 1]
        for h in range(half):
            sacc[V, h] = sacc[V, h] + sum(dot_tl(wk[h, j], kv[j, V, h]) for j in near_slots)
            for b in range(2):
                attend(b, h, [j for j in near_slots if j >= b], False)

    @pl.when(sends_val)
    def _():
        send_state(V)

    await_far(V)
    finish(V, sv)

    for b in range(2):
        for h in range(half):
            i = b * half + h
            low = xs[i].astype(BF16)
            p = ((mix[i] * nrm[i][0:1, :]) * dot_t(low, kv[window + b, K, h])).astype(BF16)
            mesa = leads[i] * dot(low, sv[i]) + dot(p, kv[window + b, V, h])
            hout[b, :, h * width:(h + 1) * width] = (att[i] / al[i] + mesa).astype(BF16)

    swap = remote(hout.at[1 - core], hother, h_sem.at[0], h_sem.at[1], sib, z)
    swap.start()
    w_copy.wait()
    prt[...] = dot(hout[core], w[core])
    swap.wait()

    chunk = tok // nz
    pieces = rsend.shape[1]
    cols = w.shape[2] // pieces

    def at(p):
        return pl.ds(pl.multiple_of(p * cols, cols), cols)

    prt[...] += dot(hother[...], w[1 - core])

    def partial(d, p):
        return prt[d * chunk:(d + 1) * chunk, at(p)]

    def right(d, p):
        return remote(rsend.at[d, p], rrecv.at[d, p], rs_s.at[d, p], rs_r.at[d, p], me, (z + 1) % nz)

    def left(d, p):
        return remote(lsend.at[d, p], lrecv.at[d, p], ls_s.at[d, p], ls_r.at[d, p], me, (z + nz - 1) % nz)

    def go_right(d):
        @pl.when(z < d)
        def _():
            @pl.loop(0, pieces)
            def _(p):
                @pl.when(z == 0)
                def _():
                    rsend[d, p] = partial(d, p).astype(BF16)

                @pl.when(z > 0)
                def _():
                    right(d, p).wait_recv()
                    rsend[d, p] = (partial(d, p) + rrecv[d, p].astype(F32)).astype(BF16)

                right(d, p).start()

    def go_left(d):
        @pl.when(z > d)
        def _():
            @pl.loop(0, pieces)
            def _(p):
                @pl.when(z == nz - 1)
                def _():
                    lsend[d, p] = partial(d, p).astype(BF16)

                @pl.when(z < nz - 1)
                def _():
                    left(d, p).wait_recv()
                    lsend[d, p] = (partial(d, p) + lrecv[d, p].astype(F32)).astype(BF16)

                left(d, p).start()

    @pl.when(z < nz // 2)
    def _():
        for k in range(nz - 1):
            go_right(nz - 1 - k)
            go_left(k)

    @pl.when(z >= nz // 2)
    def _():
        for k in range(nz - 1):
            go_left(k)
            go_right(nz - 1 - k)

    for d in range(nz):
        @pl.when(z == d)
        def _():
            @pl.loop(0, pieces)
            def _(p):
                total = partial(d, p)
                if d > 0:
                    right(d, p).wait_recv()
                    total = total + rrecv[d, p].astype(F32)
                if d < nz - 1:
                    left(d, p).wait_recv()
                    total = total + lrecv[d, p].astype(F32)
                out_ref[:, at(p)] = total.astype(BF16)

    for d in range(nz):
        for p in range(pieces):
            @pl.when(z < d)
            def _():
                right(d, p).wait_send()

            @pl.when(z > d)
            def _():
                left(d, p).wait_send()

    halo_each(K, lambda c: c.wait_send())
    halo_each(V, lambda c: c.wait_send())
    if relay:
        @pl.when(chip == 3)
        def _():
            for part in (K, V):
                for h in range(half):
                    for g in relayed(part, h):
                        relay_copy(g, part, h).wait_send()

    st_each(K, lambda c: c.wait_send())
    st_each(V, lambda c: c.wait_send())


def on_device(queries, keys, values, log_forget, strength, out_weight):
    tok, heads, width = queries.shape
    n, nz = lax.axis_size("seq"), lax.axis_size("head")
    half = heads // 2
    back = max(WINDOW // (2 * tok), 1)
    flat = [x.reshape(tok * heads, width) for x in (queries, keys, values)]
    model = out_weight.shape[1]
    weight = out_weight.reshape(2, half * width, model)
    chunk = tok // nz
    slots = 2 * back + 2
    chains = 2 * half
    pieces = 4
    dma = pltpu.SemaphoreType.DMA
    vmem = pl.BlockSpec(memory_space=pltpu.VMEM)
    hbm = pl.BlockSpec(memory_space=pl.ANY)
    return pl.pallas_call(
        functools.partial(kernel, n, nz, back),
        out_shape=jax.ShapeDtypeStruct((chunk, model), BF16),
        in_specs=[hbm, hbm, hbm, vmem, vmem, hbm],
        out_specs=vmem,
        scratch_shapes=[
            pltpu.VMEM((3, tok * heads, width), BF16),
            pltpu.VMEM((3, tok * heads, width), F32),
            pltpu.VMEM((3, 2, half, tok, width), BF16),
            pltpu.VMEM((2, 2 * half, tok), F32),
            pltpu.VMEM((slots, 2, half, tok, width), BF16),
            pltpu.VMEM((2, half, tok, width), BF16),
            pltpu.VMEM((n, 2 * half, tok), F32),
            pltpu.VMEM((n // 2, 2, half, width, width), BF16),
            pltpu.VMEM((2, half, width, width), BF16),
            pltpu.VMEM((2, half * width, model), BF16),
            pltpu.VMEM((chains, tok, tok), F32),
            pltpu.VMEM((half, slots, tok, width), F32),
            pltpu.VMEM((half, slots, tok, width), BF16),
            pltpu.VMEM((2, half, width, width), F32),
            pltpu.VMEM((chains, width, width), BF16),
            pltpu.VMEM((chains, width, width), BF16),
            pltpu.VMEM((3, half, width, width), F32),
            pltpu.VMEM((chains, tok, width), F32),
            pltpu.VMEM((chains, tok, width), F32),
            pltpu.VMEM((chains, tok, width), F32),
            pltpu.VMEM((chains, 8, tok), F32),
            pltpu.VMEM((chains, tok, width), F32),
            pltpu.VMEM((chains, tok, width), F32),
            pltpu.VMEM((chains, tok, width), F32),
            pltpu.VMEM((2, tok, half * width), BF16),
            pltpu.VMEM((tok, half * width), BF16),
            pltpu.VMEM((tok, model), F32),
            pltpu.VMEM((nz, pieces, chunk, model // pieces), BF16),
            pltpu.VMEM((nz, pieces, chunk, model // pieces), BF16),
            pltpu.VMEM((nz, pieces, chunk, model // pieces), BF16),
            pltpu.VMEM((nz, pieces, chunk, model // pieces), BF16),
            dma((3,)), dma(()),
            dma((back, 2, 2, half)), dma((slots, 2, half)), dma((3,)), dma(()), dma((n,)), dma((n,)),
            dma((2, n // 2)), dma((2, n // 2)), dma((2, 2, half)), dma((2,)),
            dma((nz, pieces)), dma((nz, pieces)), dma((nz, pieces)), dma((nz, pieces)),
        ],
        compiler_params=pltpu.CompilerParams(
            collective_id=0, has_side_effects=True, vmem_limit_bytes=56 * 1024 * 1024),
    )(*flat, log_forget, strength, weight)


def solution(mesh):
    in_specs = (
        P("seq", "head", None),
        P("seq", "head", None),
        P("seq", "head", None),
        P("head", "seq"),
        P("head", "seq"),
        P("head", None),
    )
    return jax.shard_map(
        on_device, mesh=mesh, in_specs=in_specs, out_specs=P(("seq", "head"), None), check_vma=False)
```

```python
import functools

import jax
import jax.numpy as jnp
from jax import lax
from jax.experimental import pallas as pl
from jax.experimental.pallas import tpu as pltpu
from jax.sharding import PartitionSpec as P

WINDOW = 1024
CG_STEPS = 6
RIDGE = 0.25
TINY = 1e-30
LOW = -1e30
LOG2E = 1.4426950408889634
MESH = pl.DeviceIdType.MESH
F32 = jnp.float32
BF16 = jnp.bfloat16
K, V, Q = 0, 1, 2


def dot(a, b):
    return lax.dot_general(a, b, (((1,), (0,)), ((), ())), preferred_element_type=F32)


def dot_t(a, b):
    return lax.dot_general(a, b, (((1,), (1,)), ((), ())), preferred_element_type=F32)


def dot_tl(a, b):
    return lax.dot_general(a, b, (((0,), (0,)), ((), ())), preferred_element_type=F32)


def kernel(
    n, nz, back,
    q_hbm, k_hbm, v_hbm, f_ref, s_ref, w_hbm, out_ref,
    raw, wide, own, fs_own, kv, qb, fs, st, stl, w, mix, wgt, wk, own_st, sk, sv, sacc, xs, rs, ds, nrm, att, am, al,
    hout, hother, prt, rsend, lsend, rrecv, lrecv,
    in_s, w_sem, kv_s, kv_r, sib_s, q_r, fs_s, fs_r, st_s, st_r, rl_s, h_sem, rs_s, rs_r, ls_s, ls_r,
):
    me = lax.axis_index("seq")
    z = lax.axis_index("head")
    chip, core = me // 2, me % 2
    sib = chip * 2 + (1 - core)
    chips = n // 2
    window = 2 * back
    half, tok, width = kv.shape[2], kv.shape[3], kv.shape[4]
    heads = 2 * half
    chains = 2 * half
    far_max = max(n - 2 * (back + 1), 0)
    relay = chips == 4 and back == 2

    loads = [pltpu.make_async_copy(ref, raw.at[i], in_s.at[i]) for i, ref in ((K, k_hbm), (V, v_hbm), (Q, q_hbm))]
    for i in (K, Q, V):
        loads[i].start()
    w_copy = pltpu.make_async_copy(w_hbm, w, w_sem)
    w_copy.start()

    barrier = pltpu.get_barrier_semaphore()
    for k in range(1, n):
        pl.semaphore_signal(barrier, inc=1, device_id=((me + k) % n, z), device_id_type=MESH)
    for k in range(1, nz):
        pl.semaphore_signal(barrier, inc=1, device_id=(me, (z + k) % nz), device_id_type=MESH)

    def spread(i):
        loads[i].wait()
        wide[i] = raw[i].astype(F32)
        for g in range(2):
            for h in range(half):
                own[i, g, h] = wide[i, pl.ds(g * half + h, tok, stride=heads), :].astype(BF16)

    for g in range(2):
        fs_own[g, :half] = f_ref[g * half:(g + 1) * half, :]
        fs_own[g, half:] = s_ref[g * half:(g + 1) * half, :]
    spread(K)
    pl.semaphore_wait(barrier, n - 1 + nz - 1)

    def remote(src, dst, s_sem, r_sem, s, h):
        return pltpu.make_async_remote_copy(
            src_ref=src, dst_ref=dst, send_sem=s_sem, recv_sem=r_sem,
            device_id=(s, h), device_id_type=MESH)

    def halo_copy(d, g, part, h):
        return remote(own.at[part, g, h], kv.at[window - 2 * d + core, part, h], kv_s.at[d - 1, g, part, h],
                      kv_r.at[window - 2 * d + core, part, h], (chip + d) * 2 + g, z)

    def straight(part, h):
        return part == V and h == half - 1

    def halo_each(part, act):
        for h in range(half):
            for d in range(back, 0, -1):
                ok = chip + d < chips
                if relay and d == 1:
                    ok = ok & ((chip != 1) | (core == 1)) if straight(part, h) else ok & (chip != 1)

                @pl.when(ok)
                def _():
                    for g in range(2):
                        act(halo_copy(d, g, part, h))

    def relay_copy(g, part, h):
        return remote(kv.at[g, part, h], kv.at[window - 2 + g, part, h], rl_s.at[g, part, h],
                      kv_r.at[window - 2 + g, part, h], me - 2, z)

    def relayed(part, h):
        return [0] if straight(part, h) else [0, 1]

    def await_kv(slot, part, h):
        remote(own.at[0, 0, 0], kv.at[slot, part, h], kv_s.at[0, 0, 0, 0], kv_r.at[slot, part, h], me, z).wait_recv()

    def sib_copy(part):
        other = 1 - core
        if part == Q:
            return remote(own.at[Q, other], qb.at[core], sib_s.at[Q], q_r, sib, z)
        return remote(own.at[part, other], kv.at[window + core, part], sib_s.at[part], sib_r(part, core), sib, z)

    def sib_r(part, c):
        return kv_r.at[window + c, part, 0]

    def fs_copy(j, owner):
        return remote(fs_own.at[j % 2], fs.at[owner], fs_s.at[j], fs_r.at[owner], j, z)

    sib_copy(K).start()
    for j in range(n):
        @pl.when((j // 2 >= chip) & (j != me))
        def _():
            fs_copy(j, me).start()
    halo_each(K, lambda c: c.start())
    spread(Q)
    sib_copy(Q).start()
    spread(V)
    sib_copy(V).start()

    row = lax.broadcasted_iota(jnp.int32, (tok, tok), 0)
    col = lax.broadcasted_iota(jnp.int32, (tok, tok), 1)
    tri = row >= col
    eye = row == col

    def to_col(r):
        return jnp.sum(jnp.where(eye, jnp.broadcast_to(r, (tok, tok)), 0.0), axis=1, keepdims=True)

    def to_row(c):
        return jnp.sum(jnp.where(eye, jnp.broadcast_to(c, (tok, tok)), 0.0), axis=0, keepdims=True)

    def sums_col(r):
        return jnp.sum(jnp.where(tri, jnp.broadcast_to(r, (tok, tok)), 0.0), axis=1, keepdims=True)

    def inv_norm(x):
        x = x.astype(F32)
        return lax.rsqrt(jnp.sum(x * x, axis=-1, keepdims=True) + 1e-6)

    def tail_of(f, s):
        return jnp.exp(jnp.sum(f, axis=1, keepdims=True) - sums_col(f)) * to_col(s)

    def decay(f):
        return jnp.exp(jnp.sum(f, axis=1, keepdims=True))

    kv[window + core, K] = own[K, core]
    kv[window + core, V] = own[V, core]
    qb[core] = own[Q, core]
    fs[me] = fs_own[core]

    def sib_wait(part):
        sib_copy(part).wait_send()
        dst = qb.at[1 - core] if part == Q else kv.at[window + 1 - core, part]
        remote(own.at[0, 0], dst, sib_s.at[0], q_r if part == Q else sib_r(part, 1 - core), sib, z).wait_recv()

    sib_wait(K)
    for j in range(n):
        @pl.when((j // 2 <= chip) & (j != me))
        def _():
            fs_copy(me, j).wait_recv()

        @pl.when((j // 2 >= chip) & (j != me))
        def _():
            fs_copy(j, me).wait_send()

    def gates(shard, h):
        at = (shard + n) % n
        both = fs[at]
        return both[h:h + 1, :], both[half + h:half + h + 1, :]

    def st_copy(part, to, owner):
        return remote(stl.at[part], st.at[owner, part], st_s.at[part, to], st_r.at[part, owner], to * 2 + core, z)

    def await_st(part, owner):
        remote(stl.at[part], st.at[owner, part], st_s.at[part, 0], st_r.at[part, owner], me, z).wait_recv()

    def st_each(part, act):
        for to in range(1, chips):
            ok = to > chip + back
            if relay and part == K and to == 2:
                ok = ok | (chip == 1)

            @pl.when(ok)
            def _():
                act(st_copy(part, to, chip))

    if relay:
        sends_key = chip < 2
    else:
        sends_key = chip + back + 1 < chips
    sends_val = chip + back + 1 < chips

    def lhs(j, h):
        k = kv[j, K, h]
        r = inv_norm(k)
        scaled = (wgt[h, j] * r) * k.astype(F32)
        wk[h, j] = scaled.astype(BF16)
        return (scaled * r).astype(BF16)

    for h in range(half):
        for b in range(2):
            f, s = gates(chip * 2 + b, h)
            wgt[h, window + b] = jnp.broadcast_to(tail_of(f, s), (tok, width))
        own_st[K, h] = dot_tl(lhs(window, h), kv[window, K, h])

    def send_state(part):
        for h in range(half):
            f, s = gates(chip * 2 + 1, h)
            left_side = lhs(window + 1, h) if part == K else wk[h, window + 1]
            stl[part, h] = (decay(f) * own_st[part, h] + dot_tl(left_side, kv[window + 1, part, h])).astype(BF16)
        st_each(part, lambda c: c.start())

    @pl.when(sends_key)
    def _():
        send_state(K)

    halo_each(V, lambda c: c.start())

    sib_wait(V)
    for h in range(half):
        own_st[V, h] = dot_tl(wk[h, window], kv[window, V, h])

    sib_wait(Q)
    leads = []
    for b in range(2):
        for h in range(half):
            i = b * half + h
            f, s = gates(chip * 2 + b, h)
            c_col = sums_col(f)
            c_row = to_row(c_col)
            r_row = to_row(inv_norm(kv[window + b, K, h]))
            mix[i] = jnp.where(tri, jnp.exp(jnp.minimum(c_col - c_row, 0.0)), 0.0) * (s * r_row * r_row)
            nrm[i] = jnp.broadcast_to(1.0 / r_row, (8, tok))
            q = qb[b, h].astype(F32)
            ds[i] = q * lax.rsqrt(jnp.sum(q * q, axis=-1, keepdims=True) + 1e-6)
            rs[i] = ds[i]
            xs[i] = jnp.zeros((tok, width), F32)
            leads.append(jnp.exp(c_col))

    for h in range(half):
        later = 1.0
        for j in range(window - 1, -1, -1):
            ok = chip * 2 + j >= window
            f, s = gates(chip * 2 - window + j, h)
            wgt[h, j] = jnp.broadcast_to(jnp.where(ok, tail_of(f, s) * later, 0.0), (tok, width))
            later = jnp.where(ok, later * decay(f), 1.0)
        sacc[2, h, 0:1] = jnp.broadcast_to(later, (1, width))

    unit = width ** (-0.5) * LOG2E

    def attend(b, h, slots, first):
        i = b * half + h
        q = qb[b, h]
        parts = []
        for slot in slots:
            sc = dot_t(q, kv[slot, K, h])
            ok = chip * 2 + slot >= window
            if slot == b:
                sc = jnp.where((col > row) & ok, sc, LOW)
            elif slot == b + window:
                sc = jnp.where(tri, sc, LOW)
            elif slot < window:
                sc = jnp.where(ok, sc, LOW)
            parts.append(sc)
        top = jnp.max(functools.reduce(jnp.maximum, parts), axis=1, keepdims=True) * unit
        if not first:
            before = am[i][:, 0:1]
            top = jnp.maximum(top, before)
        total = acc = None
        for slot, sc in zip(slots, parts):
            e = jnp.exp2(sc * unit - top)
            total = e if total is None else total + e
            pv = dot(e.astype(BF16), kv[slot, V, h])
            acc = pv if acc is None else acc + pv
        total = jnp.sum(total, axis=1, keepdims=True)
        if not first:
            shrink = jnp.exp2(before - top)
            total = total + shrink * al[i][:, 0:1]
            acc = acc + shrink * att[i]
        am[i] = jnp.broadcast_to(top, (tok, width))
        al[i] = jnp.broadcast_to(total, (tok, width))
        att[i] = acc

    for h in range(half):
        attend(0, h, [window], True)
        attend(1, h, [window, window + 1], True)

    def chip_decay(c, h):
        return decay(gates(c * 2, h)[0]) * decay(gates(c * 2 + 1, h)[0])

    def far_state(part, h):
        acc = jnp.zeros((width, width), F32)
        for c in range(far_max // 2):
            acc = jnp.where(c < chip - back, chip_decay(c, h) * acc + st[c, part, h].astype(F32), acc)
        return sacc[2, h, 0:1] * acc

    def await_far(part):
        for c in range(far_max // 2):
            @pl.when(c < chip - back)
            def _():
                await_st(part, c)

    def finish(part, out):
        for h in range(half):
            f, s = gates(chip * 2, h)
            acc = sacc[part, h] + far_state(part, h)
            out[h] = acc.astype(BF16)
            out[half + h] = (decay(f) * acc + own_st[part, h]).astype(BF16)

    def arrive(part, d, h):
        for g in range(2):
            slot = window - 2 * d + g

            @pl.when(chip >= d)
            def _():
                await_kv(slot, part, h)

            @pl.when(chip < d)
            def _():
                kv[slot, part, h] = jnp.zeros((tok, width), BF16)

    def pass_on(part, h):
        if relay:
            @pl.when(chip == 3)
            def _():
                for g in relayed(part, h):
                    relay_copy(g, part, h).start()

    for h in range(half):
        sacc[K, h] = jnp.zeros((width, width), F32)
    for d in range(back, 0, -1):
        late = relay and d == 1

        def near():
            for h in range(half):
                arrive(K, d, h)
                if d == back:
                    pass_on(K, h)
                for g in range(2):
                    j = window - 2 * d + g
                    sacc[K, h] = sacc[K, h] + dot_tl(lhs(j, h), kv[j, K, h])

        if late:
            @pl.when(chip != 2)
            def _():
                near()

            @pl.when(chip == 2)
            def _():
                await_st(K, 1)
                for h in range(half):
                    sacc[K, h] = sacc[K, h] + st[1, K, h].astype(F32)
        else:
            near()
    await_far(K)
    finish(K, sk)

    def step(_, carry):
        norms = []
        for i in range(chains):
            b, h = divmod(i, half)
            now = carry[i]
            dirn = ds[i]
            low = dirn.astype(BF16)
            k = kv[window + b, K, h]
            p = (mix[i] * dot_t(low, k)).astype(BF16)
            image = leads[i] * dot(low, sk[i]) + dot(p, k) + RIDGE * dirn
            alpha = now / jnp.maximum(jnp.sum(dirn * image, axis=-1, keepdims=True), TINY)
            xs[i] = xs[i] + alpha * dirn
            res = rs[i] - alpha * image
            rs[i] = res
            new = jnp.sum(res * res, axis=-1, keepdims=True)
            ds[i] = res + (new / jnp.maximum(now, TINY)) * dirn
            norms.append(new)
        return tuple(norms)

    start = tuple(jnp.sum(ds[i] * ds[i], axis=-1, keepdims=True) for i in range(chains))
    mid = CG_STEPS // 2
    norms = lax.fori_loop(0, mid, step, start)
    for h in range(half - 1):
        arrive(V, back, h)
        pass_on(V, h)
    lax.fori_loop(mid, CG_STEPS, step, norms)

    arrive(V, back, half - 1)
    pass_on(V, half - 1)
    for h in range(half):
        sacc[V, h] = jnp.zeros((width, width), F32)
    for d in range(back, 0, -1):
        if relay and d == 1:
            @pl.when(chip == 2)
            def _():
                for h in range(half):
                    arrive(K, 1, h)
                    for g in range(2):
                        lhs(window - 2 + g, h)
        near_slots = [window - 2 * d, window - 2 * d + 1]
        for h in range(half):
            if d < back:
                arrive(V, d, h)
            sacc[V, h] = sacc[V, h] + sum(dot_tl(wk[h, j], kv[j, V, h]) for j in near_slots)
            for b in range(2):
                attend(b, h, [j for j in near_slots if j >= b], False)

    @pl.when(sends_val)
    def _():
        send_state(V)

    await_far(V)
    finish(V, sv)

    for b in range(2):
        for h in range(half):
            i = b * half + h
            low = xs[i].astype(BF16)
            p = ((mix[i] * nrm[i][0:1, :]) * dot_t(low, kv[window + b, K, h])).astype(BF16)
            mesa = leads[i] * dot(low, sv[i]) + dot(p, kv[window + b, V, h])
            hout[b, :, h * width:(h + 1) * width] = (att[i] / al[i] + mesa).astype(BF16)

    swap = remote(hout.at[1 - core], hother, h_sem.at[0], h_sem.at[1], sib, z)
    swap.start()
    w_copy.wait()
    prt[...] = dot(hout[core], w[core])
    swap.wait()

    chunk = tok // nz
    pieces = rsend.shape[1]
    cols = w.shape[2] // pieces

    def at(p):
        return pl.ds(pl.multiple_of(p * cols, cols), cols)

    prt[...] += dot(hother[...], w[1 - core])

    def partial(d, p):
        return prt[d * chunk:(d + 1) * chunk, at(p)]

    def right(d, p):
        return remote(rsend.at[d, p], rrecv.at[d, p], rs_s.at[d, p], rs_r.at[d, p], me, (z + 1) % nz)

    def left(d, p):
        return remote(lsend.at[d, p], lrecv.at[d, p], ls_s.at[d, p], ls_r.at[d, p], me, (z + nz - 1) % nz)

    def go_right(d):
        @pl.when(z < d)
        def _():
            @pl.loop(0, pieces)
            def _(p):
                @pl.when(z == 0)
                def _():
                    rsend[d, p] = partial(d, p).astype(BF16)

                @pl.when(z > 0)
                def _():
                    right(d, p).wait_recv()
                    rsend[d, p] = (partial(d, p) + rrecv[d, p].astype(F32)).astype(BF16)

                right(d, p).start()

    def go_left(d):
        @pl.when(z > d)
        def _():
            @pl.loop(0, pieces)
            def _(p):
                @pl.when(z == nz - 1)
                def _():
                    lsend[d, p] = partial(d, p).astype(BF16)

                @pl.when(z < nz - 1)
                def _():
                    left(d, p).wait_recv()
                    lsend[d, p] = (partial(d, p) + lrecv[d, p].astype(F32)).astype(BF16)

                left(d, p).start()

    @pl.when(z < nz // 2)
    def _():
        for k in range(nz - 1):
            go_right(nz - 1 - k)
            go_left(k)

    @pl.when(z >= nz // 2)
    def _():
        for k in range(nz - 1):
            go_left(k)
            go_right(nz - 1 - k)

    for d in range(nz):
        @pl.when(z == d)
        def _():
            @pl.loop(0, pieces)
            def _(p):
                total = partial(d, p)
                if d > 0:
                    right(d, p).wait_recv()
                    total = total + rrecv[d, p].astype(F32)
                if d < nz - 1:
                    left(d, p).wait_recv()
                    total = total + lrecv[d, p].astype(F32)
                out_ref[:, at(p)] = total.astype(BF16)

    for d in range(nz):
        for p in range(pieces):
            @pl.when(z < d)
            def _():
                right(d, p).wait_send()

            @pl.when(z > d)
            def _():
                left(d, p).wait_send()

    halo_each(K, lambda c: c.wait_send())
    halo_each(V, lambda c: c.wait_send())
    if relay:
        @pl.when(chip == 3)
        def _():
            for part in (K, V):
                for h in range(half):
                    for g in relayed(part, h):
                        relay_copy(g, part, h).wait_send()

    st_each(K, lambda c: c.wait_send())
    st_each(V, lambda c: c.wait_send())


def on_device(queries, keys, values, log_forget, strength, out_weight):
    tok, heads, width = queries.shape
    n, nz = lax.axis_size("seq"), lax.axis_size("head")
    half = heads // 2
    back = max(WINDOW // (2 * tok), 1)
    flat = [x.reshape(tok * heads, width) for x in (queries, keys, values)]
    model = out_weight.shape[1]
    weight = out_weight.reshape(2, half * width, model)
    chunk = tok // nz
    slots = 2 * back + 2
    chains = 2 * half
    pieces = 4
    dma = pltpu.SemaphoreType.DMA
    vmem = pl.BlockSpec(memory_space=pltpu.VMEM)
    hbm = pl.BlockSpec(memory_space=pl.ANY)
    return pl.pallas_call(
        functools.partial(kernel, n, nz, back),
        out_shape=pltpu.VMEM((chunk, model), BF16),
        in_specs=[hbm, hbm, hbm, vmem, vmem, hbm],
        out_specs=vmem,
        scratch_shapes=[
            pltpu.VMEM((3, tok * heads, width), BF16),
            pltpu.VMEM((3, tok * heads, width), F32),
            pltpu.VMEM((3, 2, half, tok, width), BF16),
            pltpu.VMEM((2, 2 * half, tok), F32),
            pltpu.VMEM((slots, 2, half, tok, width), BF16),
            pltpu.VMEM((2, half, tok, width), BF16),
            pltpu.VMEM((n, 2 * half, tok), F32),
            pltpu.VMEM((n // 2, 2, half, width, width), BF16),
            pltpu.VMEM((2, half, width, width), BF16),
            pltpu.VMEM((2, half * width, model), BF16),
            pltpu.VMEM((chains, tok, tok), F32),
            pltpu.VMEM((half, slots, tok, width), F32),
            pltpu.VMEM((half, slots, tok, width), BF16),
            pltpu.VMEM((2, half, width, width), F32),
            pltpu.VMEM((chains, width, width), BF16),
            pltpu.VMEM((chains, width, width), BF16),
            pltpu.VMEM((3, half, width, width), F32),
            pltpu.VMEM((chains, tok, width), F32),
            pltpu.VMEM((chains, tok, width), F32),
            pltpu.VMEM((chains, tok, width), F32),
            pltpu.VMEM((chains, 8, tok), F32),
            pltpu.VMEM((chains, tok, width), F32),
            pltpu.VMEM((chains, tok, width), F32),
            pltpu.VMEM((chains, tok, width), F32),
            pltpu.VMEM((2, tok, half * width), BF16),
            pltpu.VMEM((tok, half * width), BF16),
            pltpu.VMEM((tok, model), F32),
            pltpu.VMEM((nz, pieces, chunk, model // pieces), BF16),
            pltpu.VMEM((nz, pieces, chunk, model // pieces), BF16),
            pltpu.VMEM((nz, pieces, chunk, model // pieces), BF16),
            pltpu.VMEM((nz, pieces, chunk, model // pieces), BF16),
            dma((3,)), dma(()),
            dma((back, 2, 2, half)), dma((slots, 2, half)), dma((3,)), dma(()), dma((n,)), dma((n,)),
            dma((2, n // 2)), dma((2, n // 2)), dma((2, 2, half)), dma((2,)),
            dma((nz, pieces)), dma((nz, pieces)), dma((nz, pieces)), dma((nz, pieces)),
        ],
        compiler_params=pltpu.CompilerParams(
            collective_id=0, has_side_effects=True, vmem_limit_bytes=56 * 1024 * 1024),
    )(*flat, log_forget, strength, weight)


def solution(mesh):
    in_specs = (
        P("seq", "head", None),
        P("seq", "head", None),
        P("seq", "head", None),
        P("head", "seq"),
        P("head", "seq"),
        P("head", None),
    )
    return jax.shard_map(
        on_device, mesh=mesh, in_specs=in_specs, out_specs=P(("seq", "head"), None), check_vma=False)
```

```python
import functools

import jax
import jax.numpy as jnp
from jax import lax
from jax.experimental import pallas as pl
from jax.experimental.pallas import tpu as pltpu
from jax.sharding import PartitionSpec as P

WINDOW = 1024
CG_STEPS = 6
RIDGE = 0.25
TINY = 1e-30
LOW = -1e30
LOG2E = 1.4426950408889634
MESH = pl.DeviceIdType.MESH
F32 = jnp.float32
BF16 = jnp.bfloat16
K, V, Q = 0, 1, 2


def dot(a, b):
    return lax.dot_general(a, b, (((1,), (0,)), ((), ())), preferred_element_type=F32)


def dot_t(a, b):
    return lax.dot_general(a, b, (((1,), (1,)), ((), ())), preferred_element_type=F32)


def dot_tl(a, b):
    return lax.dot_general(a, b, (((0,), (0,)), ((), ())), preferred_element_type=F32)


def kernel(
    n, nz, back,
    q_hbm, k_hbm, v_hbm, f_ref, s_ref, w_hbm, out_ref,
    raw, wide, own, fs_own, kv, qb, fs, st, stl, w, mix, wgt, wk, own_st, sk, sv, sacc, xs, rs, ds, nrm, lead, att, am, al,
    hout, hother, prt, rsend, lsend, rrecv, lrecv,
    in_s, w_sem, kv_s, kv_r, sib_s, q_r, fs_s, fs_r, st_s, st_r, rl_s, h_sem, rs_s, rs_r, ls_s, ls_r,
):
    me = lax.axis_index("seq")
    z = lax.axis_index("head")
    chip, core = me // 2, me % 2
    sib = chip * 2 + (1 - core)
    chips = n // 2
    window = 2 * back
    half, tok, width = kv.shape[2], kv.shape[3], kv.shape[4]
    heads = 2 * half
    chains = 2 * half
    far_max = max(n - 2 * (back + 1), 0)
    relay = chips == 4 and back == 2

    loads = [pltpu.make_async_copy(ref, raw.at[i], in_s.at[i]) for i, ref in ((K, k_hbm), (V, v_hbm), (Q, q_hbm))]
    for i in (K, Q, V):
        loads[i].start()
    w_copy = pltpu.make_async_copy(w_hbm, w, w_sem)
    w_copy.start()

    barrier = pltpu.get_barrier_semaphore()
    for k in range(1, n):
        pl.semaphore_signal(barrier, inc=1, device_id=((me + k) % n, z), device_id_type=MESH)
    for k in range(1, nz):
        pl.semaphore_signal(barrier, inc=1, device_id=(me, (z + k) % nz), device_id_type=MESH)

    def spread(i):
        loads[i].wait()
        wide[i] = raw[i].astype(F32)
        for g in range(2):
            for h in range(half):
                own[i, g, h] = wide[i, pl.ds(g * half + h, tok, stride=heads), :].astype(BF16)

    for g in range(2):
        fs_own[g, :half] = f_ref[g * half:(g + 1) * half, :]
        fs_own[g, half:] = s_ref[g * half:(g + 1) * half, :]
    spread(K)
    pl.semaphore_wait(barrier, n - 1 + nz - 1)

    def remote(src, dst, s_sem, r_sem, s, h):
        return pltpu.make_async_remote_copy(
            src_ref=src, dst_ref=dst, send_sem=s_sem, recv_sem=r_sem,
            device_id=(s, h), device_id_type=MESH)

    def halo_copy(d, g, part, h):
        return remote(own.at[part, g, h], kv.at[window - 2 * d + core, part, h], kv_s.at[d - 1, g, part, h],
                      kv_r.at[window - 2 * d + core, part, h], (chip + d) * 2 + g, z)

    def straight(part, h):
        return part == V and h == half - 1

    def halo_each(part, act):
        for h in range(half):
            for d in range(back, 0, -1):
                ok = chip + d < chips
                if relay and d == 1:
                    ok = ok & ((chip != 1) | (core == 1)) if straight(part, h) else ok & (chip != 1)

                @pl.when(ok)
                def _():
                    for g in range(2):
                        act(halo_copy(d, g, part, h))

    def relay_copy(g, part, h):
        return remote(kv.at[g, part, h], kv.at[window - 2 + g, part, h], rl_s.at[g, part, h],
                      kv_r.at[window - 2 + g, part, h], me - 2, z)

    def relayed(part, h):
        return [0] if straight(part, h) else [0, 1]

    def await_kv(slot, part, h):
        remote(own.at[0, 0, 0], kv.at[slot, part, h], kv_s.at[0, 0, 0, 0], kv_r.at[slot, part, h], me, z).wait_recv()

    def sib_copy(part):
        other = 1 - core
        if part == Q:
            return remote(own.at[Q, other], qb.at[core], sib_s.at[Q], q_r, sib, z)
        return remote(own.at[part, other], kv.at[window + core, part], sib_s.at[part], sib_r(part, core), sib, z)

    def sib_r(part, c):
        return kv_r.at[window + c, part, 0]

    def fs_copy(j, owner):
        return remote(fs_own.at[j % 2], fs.at[owner], fs_s.at[j], fs_r.at[owner], j, z)

    sib_copy(K).start()
    for j in range(n):
        @pl.when((j // 2 >= chip) & (j != me))
        def _():
            fs_copy(j, me).start()
    halo_each(K, lambda c: c.start())
    spread(Q)
    sib_copy(Q).start()
    spread(V)
    sib_copy(V).start()

    row = lax.broadcasted_iota(jnp.int32, (tok, tok), 0)
    col = lax.broadcasted_iota(jnp.int32, (tok, tok), 1)
    tri = row >= col
    eye = row == col

    def to_col(r):
        return jnp.sum(jnp.where(eye, jnp.broadcast_to(r, (tok, tok)), 0.0), axis=1, keepdims=True)

    def to_row(c):
        return jnp.sum(jnp.where(eye, jnp.broadcast_to(c, (tok, tok)), 0.0), axis=0, keepdims=True)

    def sums_col(r):
        return jnp.sum(jnp.where(tri, jnp.broadcast_to(r, (tok, tok)), 0.0), axis=1, keepdims=True)

    def inv_norm(x):
        x = x.astype(F32)
        return lax.rsqrt(jnp.sum(x * x, axis=-1, keepdims=True) + 1e-6)

    def tail_of(f, s):
        return jnp.exp(jnp.sum(f, axis=1, keepdims=True) - sums_col(f)) * to_col(s)

    def decay(f):
        return jnp.exp(jnp.sum(f, axis=1, keepdims=True))

    kv[window + core, K] = own[K, core]
    kv[window + core, V] = own[V, core]
    qb[core] = own[Q, core]
    fs[me] = fs_own[core]

    def sib_wait(part):
        sib_copy(part).wait_send()
        dst = qb.at[1 - core] if part == Q else kv.at[window + 1 - core, part]
        remote(own.at[0, 0], dst, sib_s.at[0], q_r if part == Q else sib_r(part, 1 - core), sib, z).wait_recv()

    sib_wait(K)
    for j in range(n):
        @pl.when((j // 2 <= chip) & (j != me))
        def _():
            fs_copy(me, j).wait_recv()

        @pl.when((j // 2 >= chip) & (j != me))
        def _():
            fs_copy(j, me).wait_send()

    def gates(shard, h):
        at = (shard + n) % n
        both = fs[at]
        return both[h:h + 1, :], both[half + h:half + h + 1, :]

    def st_copy(part, to, owner):
        return remote(stl.at[part], st.at[owner, part], st_s.at[part, to], st_r.at[part, owner], to * 2 + core, z)

    def await_st(part, owner):
        remote(stl.at[part], st.at[owner, part], st_s.at[part, 0], st_r.at[part, owner], me, z).wait_recv()

    def st_each(part, act):
        for to in range(1, chips):
            ok = to > chip + back
            if relay and part == K and to == 2:
                ok = ok | (chip == 1)

            @pl.when(ok)
            def _():
                act(st_copy(part, to, chip))

    if relay:
        sends_key = chip < 2
    else:
        sends_key = chip + back + 1 < chips
    sends_val = chip + back + 1 < chips

    def lhs(j, h):
        k = kv[j, K, h]
        r = inv_norm(k)
        scaled = (wgt[h, j] * r) * k.astype(F32)
        wk[h, j] = scaled.astype(BF16)
        return (scaled * r).astype(BF16)

    for h in range(half):
        for b in range(2):
            f, s = gates(chip * 2 + b, h)
            wgt[h, window + b] = jnp.broadcast_to(tail_of(f, s), (tok, width))
        own_st[K, h] = dot_tl(lhs(window, h), kv[window, K, h])

    def send_state(part):
        for h in range(half):
            f, s = gates(chip * 2 + 1, h)
            left_side = lhs(window + 1, h) if part == K else wk[h, window + 1]
            stl[part, h] = (decay(f) * own_st[part, h] + dot_tl(left_side, kv[window + 1, part, h])).astype(BF16)
        st_each(part, lambda c: c.start())

    @pl.when(sends_key)
    def _():
        send_state(K)

    halo_each(V, lambda c: c.start())

    sib_wait(V)
    for h in range(half):
        own_st[V, h] = dot_tl(wk[h, window], kv[window, V, h])

    sib_wait(Q)
    for b in range(2):
        for h in range(half):
            i = b * half + h
            f, s = gates(chip * 2 + b, h)
            c_col = sums_col(f)
            c_row = to_row(c_col)
            r_row = to_row(inv_norm(kv[window + b, K, h]))
            mix[i] = jnp.where(tri, jnp.exp(jnp.minimum(c_col - c_row, 0.0)), 0.0) * (s * r_row * r_row)
            nrm[i] = jnp.broadcast_to(1.0 / r_row, (8, tok))
            q = qb[b, h].astype(F32)
            ds[i] = q * lax.rsqrt(jnp.sum(q * q, axis=-1, keepdims=True) + 1e-6)
            rs[i] = ds[i]
            xs[i] = jnp.zeros((tok, width), F32)
            lead[i] = jnp.broadcast_to(jnp.exp(c_col), (tok, width))

    for h in range(half):
        later = 1.0
        for j in range(window - 1, -1, -1):
            ok = chip * 2 + j >= window
            f, s = gates(chip * 2 - window + j, h)
            wgt[h, j] = jnp.broadcast_to(jnp.where(ok, tail_of(f, s) * later, 0.0), (tok, width))
            later = jnp.where(ok, later * decay(f), 1.0)
        sacc[2, h, 0:1] = jnp.broadcast_to(later, (1, width))

    unit = width ** (-0.5) * LOG2E

    def attend(b, h, slots, first):
        i = b * half + h
        q = qb[b, h]
        parts = []
        for slot in slots:
            sc = dot_t(q, kv[slot, K, h])
            ok = chip * 2 + slot >= window
            if slot == b:
                sc = jnp.where((col > row) & ok, sc, LOW)
            elif slot == b + window:
                sc = jnp.where(tri, sc, LOW)
            elif slot < window:
                sc = jnp.where(ok, sc, LOW)
            parts.append(sc)
        top = jnp.max(functools.reduce(jnp.maximum, parts), axis=1, keepdims=True) * unit
        if not first:
            before = am[i][:, 0:1]
            top = jnp.maximum(top, before)
        total = acc = None
        for slot, sc in zip(slots, parts):
            e = jnp.exp2(sc * unit - top)
            total = e if total is None else total + e
            pv = dot(e.astype(BF16), kv[slot, V, h])
            acc = pv if acc is None else acc + pv
        total = jnp.sum(total, axis=1, keepdims=True)
        if not first:
            shrink = jnp.exp2(before - top)
            total = total + shrink * al[i][:, 0:1]
            acc = acc + shrink * att[i]
        am[i] = jnp.broadcast_to(top, (tok, width))
        al[i] = jnp.broadcast_to(total, (tok, width))
        att[i] = acc

    for h in range(half):
        attend(0, h, [window], True)
        attend(1, h, [window, window + 1], True)

    def chip_decay(c, h):
        return decay(gates(c * 2, h)[0]) * decay(gates(c * 2 + 1, h)[0])

    def far_state(part, h):
        acc = jnp.zeros((width, width), F32)
        for c in range(far_max // 2):
            acc = jnp.where(c < chip - back, chip_decay(c, h) * acc + st[c, part, h].astype(F32), acc)
        return sacc[2, h, 0:1] * acc

    def await_far(part):
        for c in range(far_max // 2):
            @pl.when(c < chip - back)
            def _():
                await_st(part, c)

    def finish(part, out):
        for h in range(half):
            f, s = gates(chip * 2, h)
            acc = sacc[part, h] + far_state(part, h)
            out[h] = acc.astype(BF16)
            out[half + h] = (decay(f) * acc + own_st[part, h]).astype(BF16)

    def arrive(part, d, h):
        for g in range(2):
            slot = window - 2 * d + g

            @pl.when(chip >= d)
            def _():
                await_kv(slot, part, h)

            @pl.when(chip < d)
            def _():
                kv[slot, part, h] = jnp.zeros((tok, width), BF16)

    def pass_on(part, h):
        if relay:
            @pl.when(chip == 3)
            def _():
                for g in relayed(part, h):
                    relay_copy(g, part, h).start()

    for h in range(half):
        sacc[K, h] = jnp.zeros((width, width), F32)
    for d in range(back, 0, -1):
        late = relay and d == 1

        def near():
            for h in range(half):
                arrive(K, d, h)
                if d == back:
                    pass_on(K, h)
                for g in range(2):
                    j = window - 2 * d + g
                    sacc[K, h] = sacc[K, h] + dot_tl(lhs(j, h), kv[j, K, h])

        if late:
            @pl.when(chip != 2)
            def _():
                near()

            @pl.when(chip == 2)
            def _():
                await_st(K, 1)
                for h in range(half):
                    sacc[K, h] = sacc[K, h] + st[1, K, h].astype(F32)
        else:
            near()
    await_far(K)
    finish(K, sk)

    def step(_, carry):
        norms = list(carry)
        for first in range(0, chains, 2):
            group = range(first, first + 2)
            keys = [kv[window + i // half, K, i % half] for i in group]
            lows = [ds[i].astype(BF16) for i in group]
            corrs = [dot_t(low, k) for low, k in zip(lows, keys)]
            carried = [dot(low, sk[i]) for low, i in zip(lows, group)]
            ps = [(mix[i] * corr).astype(BF16) for corr, i in zip(corrs, group)]
            images = [dot(p, k) for p, k in zip(ps, keys)]
            for at, i in enumerate(group):
                now = carry[i]
                dirn = ds[i]
                image = images[at] + lead[i] * carried[at] + RIDGE * dirn
                alpha = now / jnp.maximum(jnp.sum(dirn * image, axis=-1, keepdims=True), TINY)
                xs[i] = xs[i] + alpha * dirn
                res = rs[i] - alpha * image
                rs[i] = res
                norms[i] = jnp.sum(res * res, axis=-1, keepdims=True)
                ds[i] = res + (norms[i] / jnp.maximum(now, TINY)) * dirn
        return tuple(norms)

    start = tuple(jnp.sum(ds[i] * ds[i], axis=-1, keepdims=True) for i in range(chains))
    mid = CG_STEPS // 2
    norms = start
    for t in range(mid):
        norms = step(t, norms)
    for h in range(half - 1):
        arrive(V, back, h)
        pass_on(V, h)
    for t in range(mid, CG_STEPS):
        norms = step(t, norms)

    arrive(V, back, half - 1)
    pass_on(V, half - 1)
    for h in range(half):
        sacc[V, h] = jnp.zeros((width, width), F32)
    for d in range(back, 0, -1):
        if relay and d == 1:
            @pl.when(chip == 2)
            def _():
                for h in range(half):
                    arrive(K, 1, h)
                    for g in range(2):
                        lhs(window - 2 + g, h)
        near_slots = [window - 2 * d, window - 2 * d + 1]
        for h in range(half):
            if d < back:
                arrive(V, d, h)
            sacc[V, h] = sacc[V, h] + sum(dot_tl(wk[h, j], kv[j, V, h]) for j in near_slots)
            for b in range(2):
                attend(b, h, [j for j in near_slots if j >= b], False)

    @pl.when(sends_val)
    def _():
        send_state(V)

    await_far(V)
    finish(V, sv)

    def emit(b):
        for h in range(half):
            i = b * half + h
            low = xs[i].astype(BF16)
            p = ((mix[i] * nrm[i][0:1, :]) * dot_t(low, kv[window + b, K, h])).astype(BF16)
            mesa = lead[i] * dot(low, sv[i]) + dot(p, kv[window + b, V, h])
            hout[b, :, h * width:(h + 1) * width] = (att[i] / al[i] + mesa).astype(BF16)

    emit(1 - core)
    swap = remote(hout.at[1 - core], hother, h_sem.at[0], h_sem.at[1], sib, z)
    swap.start()
    emit(core)
    w_copy.wait()
    prt[...] = dot(hout[core], w[core])
    swap.wait()

    chunk = tok // nz
    pieces = rsend.shape[1]
    cols = w.shape[2] // pieces

    def at(p):
        return pl.ds(pl.multiple_of(p * cols, cols), cols)

    prt[...] += dot(hother[...], w[1 - core])

    def partial(d, p):
        return prt[d * chunk:(d + 1) * chunk, at(p)]

    def right(d, p):
        return remote(rsend.at[d, p], rrecv.at[d, p], rs_s.at[d, p], rs_r.at[d, p], me, (z + 1) % nz)

    def left(d, p):
        return remote(lsend.at[d, p], lrecv.at[d, p], ls_s.at[d, p], ls_r.at[d, p], me, (z + nz - 1) % nz)

    def go_right(d):
        @pl.when(z < d)
        def _():
            @pl.loop(0, pieces)
            def _(p):
                @pl.when(z == 0)
                def _():
                    rsend[d, p] = partial(d, p).astype(BF16)

                @pl.when(z > 0)
                def _():
                    right(d, p).wait_recv()
                    rsend[d, p] = (partial(d, p) + rrecv[d, p].astype(F32)).astype(BF16)

                right(d, p).start()

    def go_left(d):
        @pl.when(z > d)
        def _():
            @pl.loop(0, pieces)
            def _(p):
                @pl.when(z == nz - 1)
                def _():
                    lsend[d, p] = partial(d, p).astype(BF16)

                @pl.when(z < nz - 1)
                def _():
                    left(d, p).wait_recv()
                    lsend[d, p] = (partial(d, p) + lrecv[d, p].astype(F32)).astype(BF16)

                left(d, p).start()

    @pl.when(z < nz // 2)
    def _():
        for k in range(nz - 1):
            go_right(nz - 1 - k)
            go_left(k)

    @pl.when(z >= nz // 2)
    def _():
        for k in range(nz - 1):
            go_left(k)
            go_right(nz - 1 - k)

    for d in range(nz):
        @pl.when(z == d)
        def _():
            @pl.loop(0, pieces)
            def _(p):
                total = partial(d, p)
                if d > 0:
                    right(d, p).wait_recv()
                    total = total + rrecv[d, p].astype(F32)
                if d < nz - 1:
                    left(d, p).wait_recv()
                    total = total + lrecv[d, p].astype(F32)
                out_ref[:, at(p)] = total.astype(BF16)

    for d in range(nz):
        for p in range(pieces):
            @pl.when(z < d)
            def _():
                right(d, p).wait_send()

            @pl.when(z > d)
            def _():
                left(d, p).wait_send()

    halo_each(K, lambda c: c.wait_send())
    halo_each(V, lambda c: c.wait_send())
    if relay:
        @pl.when(chip == 3)
        def _():
            for part in (K, V):
                for h in range(half):
                    for g in relayed(part, h):
                        relay_copy(g, part, h).wait_send()

    st_each(K, lambda c: c.wait_send())
    st_each(V, lambda c: c.wait_send())


def on_device(queries, keys, values, log_forget, strength, out_weight):
    tok, heads, width = queries.shape
    n, nz = lax.axis_size("seq"), lax.axis_size("head")
    half = heads // 2
    back = max(WINDOW // (2 * tok), 1)
    flat = [x.reshape(tok * heads, width) for x in (queries, keys, values)]
    model = out_weight.shape[1]
    weight = out_weight.reshape(2, half * width, model)
    chunk = tok // nz
    slots = 2 * back + 2
    chains = 2 * half
    pieces = 4
    dma = pltpu.SemaphoreType.DMA
    vmem = pl.BlockSpec(memory_space=pltpu.VMEM)
    hbm = pl.BlockSpec(memory_space=pl.ANY)
    return pl.pallas_call(
        functools.partial(kernel, n, nz, back),
        out_shape=pltpu.VMEM((chunk, model), BF16),
        in_specs=[hbm, hbm, hbm, vmem, vmem, hbm],
        out_specs=vmem,
        scratch_shapes=[
            pltpu.VMEM((3, tok * heads, width), BF16),
            pltpu.VMEM((3, tok * heads, width), F32),
            pltpu.VMEM((3, 2, half, tok, width), BF16),
            pltpu.VMEM((2, 2 * half, tok), F32),
            pltpu.VMEM((slots, 2, half, tok, width), BF16),
            pltpu.VMEM((2, half, tok, width), BF16),
            pltpu.VMEM((n, 2 * half, tok), F32),
            pltpu.VMEM((n // 2, 2, half, width, width), BF16),
            pltpu.VMEM((2, half, width, width), BF16),
            pltpu.VMEM((2, half * width, model), BF16),
            pltpu.VMEM((chains, tok, tok), F32),
            pltpu.VMEM((half, slots, tok, width), F32),
            pltpu.VMEM((half, slots, tok, width), BF16),
            pltpu.VMEM((2, half, width, width), F32),
            pltpu.VMEM((chains, width, width), BF16),
            pltpu.VMEM((chains, width, width), BF16),
            pltpu.VMEM((3, half, width, width), F32),
            pltpu.VMEM((chains, tok, width), F32),
            pltpu.VMEM((chains, tok, width), F32),
            pltpu.VMEM((chains, tok, width), F32),
            pltpu.VMEM((chains, 8, tok), F32),
            pltpu.VMEM((chains, tok, width), F32),
            pltpu.VMEM((chains, tok, width), F32),
            pltpu.VMEM((chains, tok, width), F32),
            pltpu.VMEM((chains, tok, width), F32),
            pltpu.VMEM((2, tok, half * width), BF16),
            pltpu.VMEM((tok, half * width), BF16),
            pltpu.VMEM((tok, model), F32),
            pltpu.VMEM((nz, pieces, chunk, model // pieces), BF16),
            pltpu.VMEM((nz, pieces, chunk, model // pieces), BF16),
            pltpu.VMEM((nz, pieces, chunk, model // pieces), BF16),
            pltpu.VMEM((nz, pieces, chunk, model // pieces), BF16),
            dma((3,)), dma(()),
            dma((back, 2, 2, half)), dma((slots, 2, half)), dma((3,)), dma(()), dma((n,)), dma((n,)),
            dma((2, n // 2)), dma((2, n // 2)), dma((2, 2, half)), dma((2,)),
            dma((nz, pieces)), dma((nz, pieces)), dma((nz, pieces)), dma((nz, pieces)),
        ],
        compiler_params=pltpu.CompilerParams(
            collective_id=0, has_side_effects=True, vmem_limit_bytes=56 * 1024 * 1024),
    )(*flat, log_forget, strength, weight)


def solution(mesh):
    in_specs = (
        P("seq", "head", None),
        P("seq", "head", None),
        P("seq", "head", None),
        P("head", "seq"),
        P("head", "seq"),
        P("head", None),
    )
    return jax.shard_map(
        on_device, mesh=mesh, in_specs=in_specs, out_specs=P(("seq", "head"), None), check_vma=False)
```

```python
import functools

import jax
import jax.numpy as jnp
from jax import lax
from jax.experimental import pallas as pl
from jax.experimental.pallas import tpu as pltpu
from jax.sharding import PartitionSpec as P

WINDOW = 1024
CG_STEPS = 6
RIDGE = 0.25
TINY = 1e-30
LOW = -1e30
LOG2E = 1.4426950408889634
MESH = pl.DeviceIdType.MESH
F32 = jnp.float32
BF16 = jnp.bfloat16
K, V, Q = 0, 1, 2


def dot(a, b):
    return lax.dot_general(a, b, (((1,), (0,)), ((), ())), preferred_element_type=F32)


def dot_t(a, b):
    return lax.dot_general(a, b, (((1,), (1,)), ((), ())), preferred_element_type=F32)


def dot_tl(a, b):
    return lax.dot_general(a, b, (((0,), (0,)), ((), ())), preferred_element_type=F32)


def kernel(
    n, nz, back,
    q_hbm, k_hbm, v_hbm, f_ref, s_ref, w_hbm, out_ref,
    raw, wide, own, fs_own, kv, qb, fs, st, stl, w, mix, wgt, wk, own_st, sk, sv, sacc, xs, rs, ds, nrm, lead, att, am, al,
    hout, hother, prt, wl, hl, rsend, lsend, rrecv, lrecv,
    in_s, w_sem, kv_s, kv_r, sib_s, q_r, fs_s, fs_r, st_s, st_r, rl_s, h_sem, rs_s, rs_r, ls_s, ls_r, wl_s, wl_r, hl_s, hl_r,
):
    me = lax.axis_index("seq")
    z = lax.axis_index("head")
    chip, core = me // 2, me % 2
    sib = chip * 2 + (1 - core)
    chips = n // 2
    window = 2 * back
    half, tok, width = kv.shape[2], kv.shape[3], kv.shape[4]
    heads = 2 * half
    chains = 2 * half
    far_max = max(n - 2 * (back + 1), 0)
    relay = chips == 4 and back == 2

    loads = [pltpu.make_async_copy(ref, raw.at[i], in_s.at[i]) for i, ref in ((K, k_hbm), (V, v_hbm), (Q, q_hbm))]
    for i in (K, Q, V):
        loads[i].start()
    w_copy = pltpu.make_async_copy(w_hbm, w, w_sem)
    w_copy.start()

    barrier = pltpu.get_barrier_semaphore()
    for k in range(1, n):
        pl.semaphore_signal(barrier, inc=1, device_id=((me + k) % n, z), device_id_type=MESH)
    for k in range(1, nz):
        pl.semaphore_signal(barrier, inc=1, device_id=(me, (z + k) % nz), device_id_type=MESH)
        pl.semaphore_signal(barrier, inc=1, device_id=(sib, (z + k) % nz), device_id_type=MESH)

    def spread(i):
        loads[i].wait()
        wide[i] = raw[i].astype(F32)
        for g in range(2):
            for h in range(half):
                own[i, g, h] = wide[i, pl.ds(g * half + h, tok, stride=heads), :].astype(BF16)

    for g in range(2):
        fs_own[g, :half] = f_ref[g * half:(g + 1) * half, :]
        fs_own[g, half:] = s_ref[g * half:(g + 1) * half, :]
    spread(K)
    pl.semaphore_wait(barrier, n - 1 + 2 * (nz - 1))

    def remote(src, dst, s_sem, r_sem, s, h):
        return pltpu.make_async_remote_copy(
            src_ref=src, dst_ref=dst, send_sem=s_sem, recv_sem=r_sem,
            device_id=(s, h), device_id_type=MESH)

    def halo_copy(d, g, part, h):
        return remote(own.at[part, g, h], kv.at[window - 2 * d + core, part, h], kv_s.at[d - 1, g, part, h],
                      kv_r.at[window - 2 * d + core, part, h], (chip + d) * 2 + g, z)

    def straight(part, h):
        return part == V and h == half - 1

    def halo_each(part, act):
        for h in range(half):
            for d in range(back, 0, -1):
                ok = chip + d < chips
                if relay and d == 1:
                    ok = ok & ((chip != 1) | (core == 1)) if straight(part, h) else ok & (chip != 1)

                @pl.when(ok)
                def _():
                    for g in range(2):
                        act(halo_copy(d, g, part, h))

    def relay_copy(g, part, h):
        return remote(kv.at[g, part, h], kv.at[window - 2 + g, part, h], rl_s.at[g, part, h],
                      kv_r.at[window - 2 + g, part, h], me - 2, z)

    def relayed(part, h):
        return [0] if straight(part, h) else [0, 1]

    def await_kv(slot, part, h):
        remote(own.at[0, 0, 0], kv.at[slot, part, h], kv_s.at[0, 0, 0, 0], kv_r.at[slot, part, h], me, z).wait_recv()

    def sib_copy(part):
        other = 1 - core
        if part == Q:
            return remote(own.at[Q, other], qb.at[core], sib_s.at[Q], q_r, sib, z)
        return remote(own.at[part, other], kv.at[window + core, part], sib_s.at[part], sib_r(part, core), sib, z)

    def sib_r(part, c):
        return kv_r.at[window + c, part, 0]

    def fs_copy(j, owner):
        return remote(fs_own.at[j % 2], fs.at[owner], fs_s.at[j], fs_r.at[owner], j, z)

    chunk = tok // nz
    pieces = rsend.shape[1]
    cols = w.shape[2] // pieces
    lent = wl.shape[2] // cols
    ends = ((0, 1), (nz - 1, nz - 2)) if nz >= 4 else ()

    def lend_copy(to):
        return remote(w_hbm.at[core, :, pl.ds(0, lent * cols)], wl.at[core], wl_s.at[0], wl_r.at[core], me, to)

    def share_copy():
        return remote(wl.at[core], wl.at[core], wl_s.at[1], wl_r.at[core], sib, z)

    def await_lent(g):
        remote(wl.at[g], wl.at[g], wl_s.at[0], wl_r.at[g], me, z).wait_recv()

    def rows_of(d):
        return pl.ds(d * chunk, chunk)

    def heads_copy(b, d, to):
        return remote(hout.at[b, rows_of(d)], hl.at[core, rows_of(d)], hl_s.at[b, d], hl_r.at[core, d],
                      chip * 2 + b, to)

    def heads_far(b):
        for end, to in ends:
            @pl.when(z == end)
            def _():
                heads_copy(b, nz - 1 - end, to).start()

    sib_copy(K).start()
    for end, to in ends:
        @pl.when(z == end)
        def _():
            lend_copy(to).start()
    for j in range(n):
        @pl.when((j // 2 >= chip) & (j != me))
        def _():
            fs_copy(j, me).start()
    halo_each(K, lambda c: c.start())
    spread(Q)
    sib_copy(Q).start()
    spread(V)
    sib_copy(V).start()

    row = lax.broadcasted_iota(jnp.int32, (tok, tok), 0)
    col = lax.broadcasted_iota(jnp.int32, (tok, tok), 1)
    tri = row >= col
    eye = row == col

    def to_col(r):
        return jnp.sum(jnp.where(eye, jnp.broadcast_to(r, (tok, tok)), 0.0), axis=1, keepdims=True)

    def to_row(c):
        return jnp.sum(jnp.where(eye, jnp.broadcast_to(c, (tok, tok)), 0.0), axis=0, keepdims=True)

    def sums_col(r):
        return jnp.sum(jnp.where(tri, jnp.broadcast_to(r, (tok, tok)), 0.0), axis=1, keepdims=True)

    def inv_norm(x):
        x = x.astype(F32)
        return lax.rsqrt(jnp.sum(x * x, axis=-1, keepdims=True) + 1e-6)

    def tail_of(f, s):
        return jnp.exp(jnp.sum(f, axis=1, keepdims=True) - sums_col(f)) * to_col(s)

    def decay(f):
        return jnp.exp(jnp.sum(f, axis=1, keepdims=True))

    kv[window + core, K] = own[K, core]
    kv[window + core, V] = own[V, core]
    qb[core] = own[Q, core]
    fs[me] = fs_own[core]

    def sib_wait(part):
        sib_copy(part).wait_send()
        dst = qb.at[1 - core] if part == Q else kv.at[window + 1 - core, part]
        remote(own.at[0, 0], dst, sib_s.at[0], q_r if part == Q else sib_r(part, 1 - core), sib, z).wait_recv()

    sib_wait(K)
    for j in range(n):
        @pl.when((j // 2 <= chip) & (j != me))
        def _():
            fs_copy(me, j).wait_recv()

        @pl.when((j // 2 >= chip) & (j != me))
        def _():
            fs_copy(j, me).wait_send()

    def gates(shard, h):
        at = (shard + n) % n
        both = fs[at]
        return both[h:h + 1, :], both[half + h:half + h + 1, :]

    def st_copy(part, to, owner):
        return remote(stl.at[part], st.at[owner, part], st_s.at[part, to], st_r.at[part, owner], to * 2 + core, z)

    def await_st(part, owner):
        remote(stl.at[part], st.at[owner, part], st_s.at[part, 0], st_r.at[part, owner], me, z).wait_recv()

    def st_each(part, act):
        for to in range(1, chips):
            ok = to > chip + back
            if relay and part == K and to == 2:
                ok = ok | (chip == 1)

            @pl.when(ok)
            def _():
                act(st_copy(part, to, chip))

    if relay:
        sends_key = chip < 2
    else:
        sends_key = chip + back + 1 < chips
    sends_val = chip + back + 1 < chips

    def lhs(j, h):
        k = kv[j, K, h]
        r = inv_norm(k)
        scaled = (wgt[h, j] * r) * k.astype(F32)
        wk[h, j] = scaled.astype(BF16)
        return (scaled * r).astype(BF16)

    for h in range(half):
        for b in range(2):
            f, s = gates(chip * 2 + b, h)
            wgt[h, window + b] = jnp.broadcast_to(tail_of(f, s), (tok, width))
        own_st[K, h] = dot_tl(lhs(window, h), kv[window, K, h])

    def send_state(part):
        for h in range(half):
            f, s = gates(chip * 2 + 1, h)
            left_side = lhs(window + 1, h) if part == K else wk[h, window + 1]
            stl[part, h] = (decay(f) * own_st[part, h] + dot_tl(left_side, kv[window + 1, part, h])).astype(BF16)
        st_each(part, lambda c: c.start())

    @pl.when(sends_key)
    def _():
        send_state(K)

    halo_each(V, lambda c: c.start())

    sib_wait(V)
    for h in range(half):
        own_st[V, h] = dot_tl(wk[h, window], kv[window, V, h])

    sib_wait(Q)
    for b in range(2):
        for h in range(half):
            i = b * half + h
            f, s = gates(chip * 2 + b, h)
            c_col = sums_col(f)
            c_row = to_row(c_col)
            r_row = to_row(inv_norm(kv[window + b, K, h]))
            mix[i] = jnp.where(tri, jnp.exp(jnp.minimum(c_col - c_row, 0.0)), 0.0) * (s * r_row * r_row)
            nrm[i] = jnp.broadcast_to(1.0 / r_row, (8, tok))
            q = qb[b, h].astype(F32)
            ds[i] = q * lax.rsqrt(jnp.sum(q * q, axis=-1, keepdims=True) + 1e-6)
            rs[i] = ds[i]
            xs[i] = jnp.zeros((tok, width), F32)
            lead[i] = jnp.broadcast_to(jnp.exp(c_col), (tok, width))

    for h in range(half):
        later = 1.0
        for j in range(window - 1, -1, -1):
            ok = chip * 2 + j >= window
            f, s = gates(chip * 2 - window + j, h)
            wgt[h, j] = jnp.broadcast_to(jnp.where(ok, tail_of(f, s) * later, 0.0), (tok, width))
            later = jnp.where(ok, later * decay(f), 1.0)
        sacc[2, h, 0:1] = jnp.broadcast_to(later, (1, width))

    unit = width ** (-0.5) * LOG2E

    def attend(b, h, slots, first):
        i = b * half + h
        q = qb[b, h]
        parts = []
        for slot in slots:
            sc = dot_t(q, kv[slot, K, h])
            ok = chip * 2 + slot >= window
            if slot == b:
                sc = jnp.where((col > row) & ok, sc, LOW)
            elif slot == b + window:
                sc = jnp.where(tri, sc, LOW)
            elif slot < window:
                sc = jnp.where(ok, sc, LOW)
            parts.append(sc)
        top = jnp.max(functools.reduce(jnp.maximum, parts), axis=1, keepdims=True) * unit
        if not first:
            before = am[i][:, 0:1]
            top = jnp.maximum(top, before)
        total = acc = None
        for slot, sc in zip(slots, parts):
            e = jnp.exp2(sc * unit - top)
            total = e if total is None else total + e
            pv = dot(e.astype(BF16), kv[slot, V, h])
            acc = pv if acc is None else acc + pv
        total = jnp.sum(total, axis=1, keepdims=True)
        if not first:
            shrink = jnp.exp2(before - top)
            total = total + shrink * al[i][:, 0:1]
            acc = acc + shrink * att[i]
        am[i] = jnp.broadcast_to(top, (tok, width))
        al[i] = jnp.broadcast_to(total, (tok, width))
        att[i] = acc

    for h in range(half):
        attend(0, h, [window], True)
        attend(1, h, [window, window + 1], True)

    def chip_decay(c, h):
        return decay(gates(c * 2, h)[0]) * decay(gates(c * 2 + 1, h)[0])

    def far_state(part, h):
        acc = jnp.zeros((width, width), F32)
        for c in range(far_max // 2):
            acc = jnp.where(c < chip - back, chip_decay(c, h) * acc + st[c, part, h].astype(F32), acc)
        return sacc[2, h, 0:1] * acc

    def await_far(part):
        for c in range(far_max // 2):
            @pl.when(c < chip - back)
            def _():
                await_st(part, c)

    def finish(part, out):
        for h in range(half):
            f, s = gates(chip * 2, h)
            acc = sacc[part, h] + far_state(part, h)
            out[h] = acc.astype(BF16)
            out[half + h] = (decay(f) * acc + own_st[part, h]).astype(BF16)

    def arrive(part, d, h):
        for g in range(2):
            slot = window - 2 * d + g

            @pl.when(chip >= d)
            def _():
                await_kv(slot, part, h)

            @pl.when(chip < d)
            def _():
                kv[slot, part, h] = jnp.zeros((tok, width), BF16)

    def pass_on(part, h):
        if relay:
            @pl.when(chip == 3)
            def _():
                for g in relayed(part, h):
                    relay_copy(g, part, h).start()

    for h in range(half):
        sacc[K, h] = jnp.zeros((width, width), F32)
    for d in range(back, 0, -1):
        late = relay and d == 1

        def near():
            for h in range(half):
                arrive(K, d, h)
                if d == back:
                    pass_on(K, h)
                for g in range(2):
                    j = window - 2 * d + g
                    sacc[K, h] = sacc[K, h] + dot_tl(lhs(j, h), kv[j, K, h])

        if late:
            @pl.when(chip != 2)
            def _():
                near()

            @pl.when(chip == 2)
            def _():
                await_st(K, 1)
                for h in range(half):
                    sacc[K, h] = sacc[K, h] + st[1, K, h].astype(F32)
        else:
            near()
    await_far(K)
    finish(K, sk)

    def step(_, carry):
        norms = list(carry)
        for first in range(0, chains, 2):
            group = range(first, first + 2)
            keys = [kv[window + i // half, K, i % half] for i in group]
            lows = [ds[i].astype(BF16) for i in group]
            corrs = [dot_t(low, k) for low, k in zip(lows, keys)]
            carried = [dot(low, sk[i]) for low, i in zip(lows, group)]
            ps = [(mix[i] * corr).astype(BF16) for corr, i in zip(corrs, group)]
            images = [dot(p, k) for p, k in zip(ps, keys)]
            for at, i in enumerate(group):
                now = carry[i]
                dirn = ds[i]
                image = images[at] + lead[i] * carried[at] + RIDGE * dirn
                alpha = now / jnp.maximum(jnp.sum(dirn * image, axis=-1, keepdims=True), TINY)
                xs[i] = xs[i] + alpha * dirn
                res = rs[i] - alpha * image
                rs[i] = res
                norms[i] = jnp.sum(res * res, axis=-1, keepdims=True)
                ds[i] = res + (norms[i] / jnp.maximum(now, TINY)) * dirn
        return tuple(norms)

    start = tuple(jnp.sum(ds[i] * ds[i], axis=-1, keepdims=True) for i in range(chains))
    mid = CG_STEPS // 2
    norms = start
    for t in range(mid):
        norms = step(t, norms)
    for h in range(half - 1):
        arrive(V, back, h)
        pass_on(V, h)
    for t in range(mid, CG_STEPS):
        norms = step(t, norms)

    arrive(V, back, half - 1)
    pass_on(V, half - 1)
    for h in range(half):
        sacc[V, h] = jnp.zeros((width, width), F32)
    for d in range(back, 0, -1):
        if relay and d == 1:
            @pl.when(chip == 2)
            def _():
                for h in range(half):
                    arrive(K, 1, h)
                    for g in range(2):
                        lhs(window - 2 + g, h)
        near_slots = [window - 2 * d, window - 2 * d + 1]
        for h in range(half):
            if d < back:
                arrive(V, d, h)
            sacc[V, h] = sacc[V, h] + sum(dot_tl(wk[h, j], kv[j, V, h]) for j in near_slots)
            for b in range(2):
                attend(b, h, [j for j in near_slots if j >= b], False)

    for end, to in ends:
        @pl.when(z == to)
        def _():
            await_lent(core)
            share_copy().start()

    @pl.when(sends_val)
    def _():
        send_state(V)

    await_far(V)
    finish(V, sv)

    def emit(b):
        for h in range(half):
            i = b * half + h
            low = xs[i].astype(BF16)
            p = ((mix[i] * nrm[i][0:1, :]) * dot_t(low, kv[window + b, K, h])).astype(BF16)
            mesa = lead[i] * dot(low, sv[i]) + dot(p, kv[window + b, V, h])
            hout[b, :, h * width:(h + 1) * width] = (att[i] / al[i] + mesa).astype(BF16)

    emit(1 - core)
    swap = remote(hout.at[1 - core], hother, h_sem.at[0], h_sem.at[1], sib, z)
    swap.start()
    heads_far(1 - core)
    emit(core)
    heads_far(core)
    w_copy.wait()
    prt[...] = dot(hout[core], w[core])
    swap.wait()

    def at(p):
        return pl.ds(pl.multiple_of(p * cols, cols), cols)

    prt[...] += dot(hother[...], w[1 - core])

    def partial(d, p):
        return prt[d * chunk:(d + 1) * chunk, at(p)]

    def right(d, p):
        return remote(rsend.at[d, p], rrecv.at[d, p], rs_s.at[d, p], rs_r.at[d, p], me, (z + 1) % nz)

    def left(d, p):
        return remote(lsend.at[d, p], lrecv.at[d, p], ls_s.at[d, p], ls_r.at[d, p], me, (z + nz - 1) % nz)

    early = (1, 0, lent) if ends else (0, 0, 0)
    rest = (0, early[2], pieces)

    def go_right(d, span):
        base, low, high = span

        @pl.when((z >= base) & (z < d))
        def _():
            if low == high:
                return

            @pl.loop(low, high)
            def _(p):
                @pl.when(z == base)
                def _():
                    rsend[d, p] = partial(d, p).astype(BF16)

                @pl.when(z > base)
                def _():
                    right(d, p).wait_recv()
                    rsend[d, p] = (partial(d, p) + rrecv[d, p].astype(F32)).astype(BF16)

                right(d, p).start()

    def go_left(d, span):
        base, low, high = span

        @pl.when((z <= nz - 1 - base) & (z > d))
        def _():
            if low == high:
                return

            @pl.loop(low, high)
            def _(p):
                @pl.when(z == nz - 1 - base)
                def _():
                    lsend[d, p] = partial(d, p).astype(BF16)

                @pl.when(z < nz - 1 - base)
                def _():
                    left(d, p).wait_recv()
                    lsend[d, p] = (partial(d, p) + lrecv[d, p].astype(F32)).astype(BF16)

                left(d, p).start()

    def absorb(d):
        for g in range(2):
            remote(hout.at[0, rows_of(d)], hl.at[g, rows_of(d)], hl_s.at[0, d], hl_r.at[g, d], me, z).wait_recv()
        prt[rows_of(d), 0:lent * cols] += dot(hl[0, rows_of(d)], wl[0]) + dot(hl[1, rows_of(d)], wl[1])

    def both(go, d):
        go(d, early)
        go(d, rest)

    for end, to in ends:
        ahead, behind = (go_right, go_left) if end == 0 else (go_left, go_right)
        order = list(range(nz - 1, 0, -1)) if end == 0 else list(range(nz - 1))

        @pl.when(z == end)
        def _():
            for d in order:
                if d != order[0]:
                    for b in range(2):
                        heads_copy(b, d, to).start()
                ahead(d, rest)

        @pl.when(z == to)
        def _():
            await_lent(1 - core)
            absorb(order[0])
            both(ahead, order[0])
            behind(end, early)
            for d in order[1:-1]:
                absorb(d)
                ahead(d, early)
                if d == order[1]:
                    behind(end, rest)
                ahead(d, rest)
            absorb(to)

    inner = (z > 1) & (z < nz - 2) if ends else z >= 0

    @pl.when(inner & (z < nz // 2))
    def _():
        for k in range(nz - 1):
            both(go_right, nz - 1 - k)
            both(go_left, k)

    @pl.when(inner & (z >= nz // 2))
    def _():
        for k in range(nz - 1):
            both(go_left, k)
            both(go_right, nz - 1 - k)

    for d in range(nz):
        @pl.when(z == d)
        def _():
            for base, low, high in (early, rest):
                if low == high:
                    continue

                @pl.loop(low, high)
                def _(p):
                    total = partial(d, p)
                    if d > base:
                        right(d, p).wait_recv()
                        total = total + rrecv[d, p].astype(F32)
                    if d < nz - 1 - base:
                        left(d, p).wait_recv()
                        total = total + lrecv[d, p].astype(F32)
                    out_ref[:, at(p)] = total.astype(BF16)

    for d in range(nz):
        for base, low, high in (early, rest):
            for p in range(low, high):
                @pl.when((z >= base) & (z < d))
                def _():
                    right(d, p).wait_send()

                @pl.when((z <= nz - 1 - base) & (z > d))
                def _():
                    left(d, p).wait_send()

    for end, to in ends:
        @pl.when(z == end)
        def _():
            lend_copy(to).wait_send()

        @pl.when(z == to)
        def _():
            share_copy().wait_send()
    for end, to in ends:
        @pl.when(z == end)
        def _():
            for b in range(2):
                for d in (range(1, nz) if end == 0 else range(nz - 1)):
                    heads_copy(b, d, to).wait_send()
    halo_each(K, lambda c: c.wait_send())
    halo_each(V, lambda c: c.wait_send())
    if relay:
        @pl.when(chip == 3)
        def _():
            for part in (K, V):
                for h in range(half):
                    for g in relayed(part, h):
                        relay_copy(g, part, h).wait_send()

    st_each(K, lambda c: c.wait_send())
    st_each(V, lambda c: c.wait_send())


def on_device(queries, keys, values, log_forget, strength, out_weight):
    tok, heads, width = queries.shape
    n, nz = lax.axis_size("seq"), lax.axis_size("head")
    half = heads // 2
    back = max(WINDOW // (2 * tok), 1)
    flat = [x.reshape(tok * heads, width) for x in (queries, keys, values)]
    model = out_weight.shape[1]
    weight = out_weight.reshape(2, half * width, model)
    chunk = tok // nz
    slots = 2 * back + 2
    chains = 2 * half
    pieces = 4
    lent = 2
    dma = pltpu.SemaphoreType.DMA
    vmem = pl.BlockSpec(memory_space=pltpu.VMEM)
    hbm = pl.BlockSpec(memory_space=pl.ANY)
    return pl.pallas_call(
        functools.partial(kernel, n, nz, back),
        out_shape=pltpu.VMEM((chunk, model), BF16),
        in_specs=[hbm, hbm, hbm, vmem, vmem, hbm],
        out_specs=vmem,
        scratch_shapes=[
            pltpu.VMEM((3, tok * heads, width), BF16),
            pltpu.VMEM((3, tok * heads, width), F32),
            pltpu.VMEM((3, 2, half, tok, width), BF16),
            pltpu.VMEM((2, 2 * half, tok), F32),
            pltpu.VMEM((slots, 2, half, tok, width), BF16),
            pltpu.VMEM((2, half, tok, width), BF16),
            pltpu.VMEM((n, 2 * half, tok), F32),
            pltpu.VMEM((n // 2, 2, half, width, width), BF16),
            pltpu.VMEM((2, half, width, width), BF16),
            pltpu.VMEM((2, half * width, model), BF16),
            pltpu.VMEM((chains, tok, tok), F32),
            pltpu.VMEM((half, slots, tok, width), F32),
            pltpu.VMEM((half, slots, tok, width), BF16),
            pltpu.VMEM((2, half, width, width), F32),
            pltpu.VMEM((chains, width, width), BF16),
            pltpu.VMEM((chains, width, width), BF16),
            pltpu.VMEM((3, half, width, width), F32),
            pltpu.VMEM((chains, tok, width), F32),
            pltpu.VMEM((chains, tok, width), F32),
            pltpu.VMEM((chains, tok, width), F32),
            pltpu.VMEM((chains, 8, tok), F32),
            pltpu.VMEM((chains, tok, width), F32),
            pltpu.VMEM((chains, tok, width), F32),
            pltpu.VMEM((chains, tok, width), F32),
            pltpu.VMEM((chains, tok, width), F32),
            pltpu.VMEM((2, tok, half * width), BF16),
            pltpu.VMEM((tok, half * width), BF16),
            pltpu.VMEM((tok, model), F32),
            pltpu.VMEM((2, half * width, lent * (model // pieces)), BF16),
            pltpu.VMEM((2, tok, half * width), BF16),
            pltpu.VMEM((nz, pieces, chunk, model // pieces), BF16),
            pltpu.VMEM((nz, pieces, chunk, model // pieces), BF16),
            pltpu.VMEM((nz, pieces, chunk, model // pieces), BF16),
            pltpu.VMEM((nz, pieces, chunk, model // pieces), BF16),
            dma((3,)), dma(()),
            dma((back, 2, 2, half)), dma((slots, 2, half)), dma((3,)), dma(()), dma((n,)), dma((n,)),
            dma((2, n // 2)), dma((2, n // 2)), dma((2, 2, half)), dma((2,)),
            dma((nz, pieces)), dma((nz, pieces)), dma((nz, pieces)), dma((nz, pieces)),
            dma((2,)), dma((2,)), dma((2, nz)), dma((2, nz)),
        ],
        compiler_params=pltpu.CompilerParams(
            collective_id=0, has_side_effects=True, vmem_limit_bytes=56 * 1024 * 1024),
    )(*flat, log_forget, strength, weight)


def solution(mesh):
    in_specs = (
        P("seq", "head", None),
        P("seq", "head", None),
        P("seq", "head", None),
        P("head", "seq"),
        P("head", "seq"),
        P("head", None),
    )
    return jax.shard_map(
        on_device, mesh=mesh, in_specs=in_specs, out_specs=P(("seq", "head"), None), check_vma=False)
```
